256 devices in a mesh: segment: 4 (over y), frame: 16 (over z, core), row: 4 (over x).
Axes of the slice: x: 4, y: 4, z: 8, core: 2. Of those that a mesh axis runs over, the one named last changes fastest.
Arguments:
- latents: bfloat16 [2, 32, 8, 24, 320], P(None, 'frame', 'row')
- cotangent: bfloat16 [2, 32, 8, 24, 320], P(None, 'frame', 'row'), may hold values from -0.0546875 to 0.0546875
- timesteps: int32 [2], replicated, may hold values from 0 to 999
- frame_counts: int32 [2], replicated, may hold values from 8 to 32, as said below
- spatial_weight: bfloat16 [4, 9, 320, 320], P('segment'), may hold values from -0.109375 to 0.109375
- temporal_weight: bfloat16 [4, 3, 320, 320], P('segment'), may hold values from -0.1875 to 0.1875
- time_weight: bfloat16 [4, 1280, 320], P('segment'), may hold values from -0.15625 to 0.15625
- norm_gain: float32 [4, 320], P('segment'), may hold values from 0.5 to 1.5
Outputs:
- spatial_grad: float32 [4, 2880, 320], P('segment', ('frame', 'row'))
- temporal_grad: float32 [4, 960, 320], P('segment', ('frame', 'row'))
- time_grad: float32 [4, 1280, 320], P('segment', ('frame', 'row'))
- gain_grad: float32 [4, 320], P('segment', ('frame', 'row'))
The draws below stay inside these ranges and needn't reach their ends.
Inputs may be any that keep to these rules, and one draw needn't show every extreme that they name: Frames frame_counts[c] and later of clip c are padding; some clip has all 32 frames.
All inputs are finite; a program needn't handle non-finite values.
Results may differ from the reference program's by a relative error of at most 0.02.
Values may be sent and summed in bfloat16 or wider, within the bound.
No kernel may reach another device: no remote copies, remote signals or barrier semaphores. Data moves between devices by JAX's collectives and lax.ppermute only.
A program may use at most 128 MiB of HBM per device.

```python
import jax
import jax.numpy as jnp
from jax import lax

C = 320
G = 32
TE = 1280
WIDTH = 24
CLIPS = 2
SECTIONS = 4
FRAMES = 32
ROWS = 8


def draw_latents(key, part):
    subkeys = jax.random.split(key, 3)
    full_shape = (CLIPS, FRAMES, ROWS, WIDTH, C)
    frame_pos = jnp.arange(FRAMES).astype(jnp.float32) / max(FRAMES - 1, 1)
    jitter = jnp.exp(jax.random.uniform(subkeys[0], (CLIPS, FRAMES, ROWS, 1, 1), minval=-0.3, maxval=0.3))
    channel_scale = 10.0 ** (jax.random.uniform(subkeys[1], (C,)) - 0.5)
    frame_scale = 10.0 ** (frame_pos - 0.5)
    cell_scale = 0.3 * frame_scale[None, :, None, None, None] * jitter * channel_scale
    values = cell_scale * jax.random.normal(subkeys[2], full_shape)
    return values.astype(jnp.bfloat16)


def draw_frame_counts(key, part):
    subkeys = jax.random.split(key, 2)
    fewest = max(1, FRAMES // 4)
    counts = jax.random.randint(subkeys[0], (CLIPS,), fewest, FRAMES + 1)
    full_clip = jax.random.randint(subkeys[1], (), 0, CLIPS)
    counts = counts.at[full_clip].set(FRAMES)
    return counts.astype(jnp.int32)


def steps_of(key, extent, pieces, low, high):
    def one(position, blocks):
        draws = jax.random.uniform(jax.random.fold_in(jax.random.fold_in(key, 6), position), (blocks,), jnp.float32, low / len(pieces), high / len(pieces))
        return jnp.repeat(jnp.exp(draws), extent[position] // blocks).reshape((-1,) + (1,) * (len(extent) - position - 1))

    level = one(*pieces[0])
    for cut in pieces[1:]:
        level = level * one(*cut)
    return level


def noise(key, dims, width, reach, pieces=(), kind=jnp.bfloat16):
    values = width * jax.random.normal(key, dims, jnp.float32)
    if pieces:
        values = values * steps_of(key, dims, pieces, -0.22, 0.18)
    return jnp.clip(values, -reach, reach).astype(kind)


def setup_inputs(seed: int = 0) -> dict:
    key_list = jax.random.split(jax.random.key(seed), 9)
    return {
        "latents": draw_latents(jax.random.fold_in(key_list[8], 71), 0),
        "cotangent": noise(key_list[1], (CLIPS, FRAMES, ROWS, WIDTH, C), (CLIPS * FRAMES * ROWS * WIDTH) ** -0.5, 0.0546875, ((1, 16), (2, 4))),
        "timesteps": jax.random.randint(key_list[2], (CLIPS,), 0, 1000).astype(jnp.int32),
        "frame_counts": draw_frame_counts(jax.random.fold_in(key_list[8], 71), 0),
        "spatial_weight": noise(key_list[4], (SECTIONS, 9, C, C), (9 * C) ** -0.5, 0.109375, ((0, 4),)),
        "temporal_weight": noise(key_list[5], (SECTIONS, 3, C, C), (3 * C) ** -0.5, 0.1875, ((0, 4),)),
        "time_weight": noise(key_list[6], (SECTIONS, TE, C), TE ** -0.5, 0.15625, ((0, 4),)),
        "norm_gain": jnp.clip(0.5 + 1.0 * jax.random.uniform(key_list[7], (SECTIONS, C), jnp.float32) ** steps_of(key_list[7], (SECTIONS, C), ((0, 4),), -0.2, 0.2), 0.5, 1.5),
    }


EPSILON = 1e-05

def time_features(timesteps):
    half_dim = TE // 2
    frequency = jnp.exp(-jnp.log(10000.0) * jnp.arange(half_dim).astype(jnp.float32) / half_dim)
    angles = timesteps.astype(jnp.float32)[:, None] * frequency[None, :]
    wave_parts = jnp.concatenate([jnp.cos(angles), jnp.sin(angles)], axis=1)
    return jax.nn.silu(wave_parts).astype(jnp.bfloat16)

def group_sum(values):
    per_channel = lax.optimization_barrier(jnp.sum(values, axis=(0, 1, 2)))
    return per_channel.reshape(G, -1).sum(axis=1)

def spread(values):
    return jnp.repeat(values, C // G)

def spatial_columns(padded, row_count, col_count):
    return jnp.concatenate([padded[:, vertical:vertical + row_count, lateral:lateral + col_count, :] for vertical in range(3) for lateral in range(3)], axis=-1)

def flip_columns(padded, row_count, col_count):
    return jnp.concatenate([padded[:, 2 - vertical:2 - vertical + row_count, 2 - lateral:2 - lateral + col_count, :] for vertical in range(3) for lateral in range(3)], axis=-1)

def time_columns(padded, frame_count):
    return jnp.concatenate([padded[offset:offset + frame_count] for offset in range(3)], axis=-1)

def time_flip(padded, frame_count):
    return jnp.concatenate([padded[2 - offset:2 - offset + frame_count] for offset in range(3)], axis=-1)

def flat_dot(columns, matrix):
    return jnp.dot(columns.reshape(-1, matrix.shape[0]), matrix, preferred_element_type=jnp.float32)

def outer_dot(columns, right_side):
    return jnp.dot(columns.reshape(-1, columns.shape[-1]).T, right_side.reshape(-1, right_side.shape[-1]), preferred_element_type=jnp.float32)

def section_forward(current, kernel, tkernel, bias_row, gain_row, frame_mask, cell_total):
    frame_count, row_count, col_count, channels = current.shape
    padded_in = jnp.pad(current, ((0, 0), (1, 1), (1, 1), (0, 0)))
    hidden = flat_dot(spatial_columns(padded_in, row_count, col_count), kernel.reshape(9 * channels, channels)).reshape(current.shape) + bias_row
    group_mean = group_sum(hidden * frame_mask) / cell_total
    centred = hidden - spread(group_mean)
    variance = group_sum(frame_mask * centred * centred) / cell_total
    inv_spread = lax.rsqrt(variance + EPSILON)
    normed = centred * spread(inv_spread)
    activated = (frame_mask * jax.nn.silu(normed * gain_row)).astype(jnp.bfloat16)
    padded_act = jnp.pad(activated, ((1, 1), (0, 0), (0, 0), (0, 0)))
    temporal = flat_dot(time_columns(padded_act, frame_count), tkernel.reshape(3 * channels, channels)).reshape(current.shape)
    output = (current.astype(jnp.float32) + temporal).astype(jnp.bfloat16)
    return (output, (padded_in, hidden, padded_act, group_mean, inv_spread))

def section_backward(upstream, stored, kernel, tkernel, gain_row, frame_mask, cell_total):
    padded_in, hidden, padded_act, group_mean, inv_spread = stored
    frame_count, row_count, col_count, channels = hidden.shape
    padded_up = jnp.pad(upstream, ((1, 1), (0, 0), (0, 0), (0, 0)))
    tkernel_back = jnp.transpose(tkernel, (0, 2, 1)).reshape(3 * channels, channels)
    act_grad = flat_dot(time_flip(padded_up, frame_count), tkernel_back).reshape(hidden.shape)
    temporal_part = outer_dot(time_columns(padded_act, frame_count), upstream)
    normed = (hidden - spread(group_mean)) * spread(inv_spread)
    scaled = normed * gain_row
    gate_sig = jax.nn.sigmoid(scaled)
    scaled_grad = act_grad * frame_mask * gate_sig * (1.0 + scaled * (1.0 - gate_sig))
    gain_part = lax.optimization_barrier(jnp.sum(scaled_grad * normed, axis=(0, 1, 2)))
    normed_grad = scaled_grad * gain_row
    first_moment = group_sum(normed_grad) / cell_total
    second_moment = group_sum(normed_grad * normed) / cell_total
    hidden_grad = (spread(inv_spread) * (normed_grad - frame_mask * (spread(first_moment) + normed * spread(second_moment)))).astype(jnp.bfloat16)
    column_sums = lax.optimization_barrier(jnp.sum(hidden_grad.astype(jnp.float32), axis=(0, 1, 2)))
    spatial_part = outer_dot(spatial_columns(padded_in, row_count, col_count), hidden_grad)
    padded_grad = jnp.pad(hidden_grad, ((0, 0), (1, 1), (1, 1), (0, 0)))
    kernel_back = jnp.transpose(kernel, (0, 2, 1)).reshape(9 * channels, channels)
    conv_back = flat_dot(flip_columns(padded_grad, row_count, col_count), kernel_back).reshape(hidden.shape)
    input_grad = (upstream.astype(jnp.float32) + conv_back).astype(jnp.bfloat16)
    return (input_grad, spatial_part, temporal_part, gain_part, column_sums)

def reference(latents, cotangent, timesteps, frame_counts, spatial_weight, temporal_weight, time_weight, norm_gain):
    sections = spatial_weight.shape[0]
    time_embed = time_features(timesteps)
    biases = [jnp.dot(time_embed, time_weight[section], preferred_element_type=jnp.float32) for section in range(sections)]
    frame_ids = jnp.arange(FRAMES).astype(jnp.int32)
    group_width = C // G
    totals = (jnp.zeros((sections, 9 * C, C), jnp.float32), jnp.zeros((sections, 3 * C, C), jnp.float32), jnp.zeros((sections, TE, C), jnp.float32), jnp.zeros((sections, C), jnp.float32))

    def one_clip(totals, clip_index):
        frame_limit = frame_counts[clip_index]
        frame_mask = (frame_ids < frame_limit).astype(jnp.float32)[:, None, None, None]
        cell_total = frame_limit.astype(jnp.float32) * ROWS * WIDTH * group_width
        stored_list = []
        current = latents[clip_index]
        skip_path = current
        for section in range(sections):
            if section == sections - 1:
                current = (current.astype(jnp.float32) + skip_path.astype(jnp.float32)).astype(jnp.bfloat16)
            current, stored = section_forward(current, spatial_weight[section], temporal_weight[section], biases[section][clip_index], norm_gain[section], frame_mask, cell_total)
            stored_list.append(stored)
            if section == 0:
                skip_path = current
        upstream = (frame_mask * cotangent[clip_index].astype(jnp.float32)).astype(jnp.bfloat16)
        skip_grad = upstream
        embed_row = time_embed[clip_index].astype(jnp.float32)
        spatial_total, temporal_total, time_total, gain_total = totals
        for section in reversed(range(sections)):
            if section == 0:
                upstream = (upstream.astype(jnp.float32) + skip_grad.astype(jnp.float32)).astype(jnp.bfloat16)
            input_grad, spatial_part, temporal_part, gain_part, column_sums = section_backward(upstream, stored_list[section], spatial_weight[section], temporal_weight[section], norm_gain[section], frame_mask, cell_total)
            spatial_total = spatial_total.at[section].add(spatial_part)
            temporal_total = temporal_total.at[section].add(temporal_part)
            time_total = time_total.at[section].add(embed_row[:, None] * column_sums[None, :])
            gain_total = gain_total.at[section].add(gain_part)
            if section == sections - 1:
                skip_grad = input_grad
            upstream = input_grad
        return ((spatial_total, temporal_total, time_total, gain_total), None)
    totals, ignored = lax.scan(one_clip, totals, jnp.arange(CLIPS).astype(jnp.int32))
    return (totals[0], totals[1], totals[2], totals[3])
```

```python
import jax
import jax.numpy as jnp
from jax import lax
from jax.sharding import PartitionSpec as P

C = 320
G = 32
TE = 1280
WIDTH = 24
R_DEV = 2
F_DEV = 2
CLIPS = 2


EPSILON = 1e-05


def with_halo(array, sides, width):
    for axis, dim in sides:
        peers, length = (lax.axis_size(axis), array.shape[dim])
        up = [(i, (i + 1) % peers) for i in range(peers - 1)]
        down = [(j, i) for i, j in up]
        last = lax.slice_in_dim(array, length - width, length, axis=dim)
        leading = lax.slice_in_dim(array, 0, width, axis=dim)
        before = lax.ppermute(last, axis, up)
        after = lax.ppermute(leading, axis, down)
        array = jnp.concatenate([before, array, after], axis=dim)
    return array


def shifted(array, axis, by):
    peers = lax.axis_size(axis)
    pairs = [(i, i + by) for i in range(peers) if 0 <= i + by < peers]
    return lax.ppermute(array, axis, pairs)


def time_features(timesteps):
    half_dim = TE // 2
    frequency = jnp.exp(-jnp.log(10000.0) * jnp.arange(half_dim).astype(jnp.float32) / half_dim)
    angles = timesteps.astype(jnp.float32)[:, None] * frequency[None, :]
    wave_parts = jnp.concatenate([jnp.cos(angles), jnp.sin(angles)], axis=1)
    return jax.nn.silu(wave_parts).astype(jnp.bfloat16)


def group_sum(values):
    per_channel = jnp.sum(values, axis=(1, 2, 3))
    return per_channel.reshape(CLIPS, G, -1).sum(axis=2)


def spread(values):
    return jnp.repeat(values, C // G, axis=-1)[:, None, None, None, :]


def spatial_columns(padded, row_count, col_count):
    return jnp.concatenate(
        [
            padded[:, :, a : a + row_count, b : b + col_count, :]
            for a in range(3)
            for b in range(3)
        ],
        axis=-1,
    )


def flip_columns(padded, row_count, col_count):
    return jnp.concatenate(
        [
            padded[:, :, 2 - a : 2 - a + row_count, 2 - b : 2 - b + col_count, :]
            for a in range(3)
            for b in range(3)
        ],
        axis=-1,
    )


def time_columns(padded, frame_count):
    return jnp.concatenate([padded[:, k : k + frame_count] for k in range(3)], axis=-1)


def time_flip(padded, frame_count):
    return jnp.concatenate([padded[:, 2 - k : 2 - k + frame_count] for k in range(3)], axis=-1)


def flat_dot(columns, matrix):
    return jnp.dot(columns.reshape(-1, matrix.shape[0]), matrix, preferred_element_type=jnp.float32)


def outer_dot(columns, right_side):
    return lax.dot_general(
        columns.reshape(-1, columns.shape[-1]),
        right_side.reshape(-1, right_side.shape[-1]),
        (((0,), (0,)), ((), ())),
        preferred_element_type=jnp.float32,
    )


def everyones(values):
    peers = lax.axis_size("frame") * lax.axis_size("row")
    sent = jnp.broadcast_to(values[None], (peers,) + values.shape)
    return lax.all_to_all(sent, ("frame", "row"), 0, 0)


def scatter_sum(partial):
    frames, rows = lax.axis_size("frame"), lax.axis_size("row")
    split = partial.reshape(frames, rows, -1, partial.shape[-1]).astype(jnp.bfloat16)
    got = lax.all_to_all(split, "row", 1, 1)
    half = jnp.sum(got.astype(jnp.float32), axis=1).astype(jnp.bfloat16)
    got = lax.all_to_all(half, "frame", 0, 0)
    return jnp.sum(got.astype(jnp.float32), axis=0)


def per_device(
    latents,
    cotangent,
    timesteps,
    frame_counts,
    spatial_weight,
    temporal_weight,
    time_weight,
    norm_gain,
):
    sections = lax.axis_size("segment")
    segment_index = lax.axis_index("segment")
    all_rows = R_DEV * lax.axis_size("row")
    group_width = C // G
    act_shape = (CLIPS, F_DEV, R_DEV, WIDTH, C)
    kernel = spatial_weight[0]
    tkernel = temporal_weight[0]
    gain_row = norm_gain[0]
    kernel_flat = kernel.reshape(9 * C, C)
    kernel_back = jnp.transpose(kernel, (0, 2, 1)).reshape(9 * C, C)
    tkernel_flat = tkernel.reshape(3 * C, C)
    tkernel_back = jnp.transpose(tkernel, (0, 2, 1)).reshape(3 * C, C)
    time_embed = time_features(timesteps)
    clip_biases = jnp.dot(time_embed, time_weight[0], preferred_element_type=jnp.float32)
    frame_ids = lax.axis_index("frame") * F_DEV + jnp.arange(F_DEV)
    frame_mask = (frame_ids[None, :] < frame_counts[:, None]).astype(jnp.float32)
    frame_mask = frame_mask[:, :, None, None, None]
    unit = float(all_rows * WIDTH * group_width)
    cell_total = (frame_counts.astype(jnp.float32) * unit)[:, None]
    starts = (jnp.arange(lax.axis_size("frame")) * F_DEV)[:, None]
    held = jnp.clip(frame_counts[None, :] - starts, 0, F_DEV).astype(jnp.float32)
    held = jnp.repeat(held * (R_DEV * WIDTH * group_width), lax.axis_size("row"), axis=0)
    held = held[:, :, None]
    mine = lax.axis_index("frame") * lax.axis_size("row")
    own_cells = jnp.maximum(lax.dynamic_index_in_dim(held, mine, 0, keepdims=False), 1.0)

    received = jnp.zeros(act_shape, jnp.bfloat16)
    skip = None
    kept = None
    for tick in range(sections):
        is_live = segment_index == tick
        current = latents if tick == 0 else received
        if tick == sections - 1:
            current = (current.astype(jnp.float32) + skip.astype(jnp.float32)).astype(jnp.bfloat16)
        padded_rows = with_halo(current, (("row", 2),), 1)
        padded_in = jnp.pad(padded_rows, ((0, 0), (0, 0), (0, 0), (1, 1), (0, 0)))
        hidden = flat_dot(spatial_columns(padded_in, R_DEV, WIDTH), kernel_flat).reshape(
            act_shape
        ) + clip_biases[:, None, None, None, :]
        own_mean = group_sum(hidden * frame_mask) / own_cells
        off = hidden - spread(own_mean)
        own_square = group_sum(frame_mask * off * off)
        gathered = everyones(jnp.stack([own_mean, own_square]))
        group_mean = jnp.sum(held * gathered[:, 0], axis=0) / cell_total
        apart = gathered[:, 0] - group_mean[None]
        variance = jnp.sum(gathered[:, 1] + held * apart * apart, axis=0) / cell_total
        inv_spread = lax.rsqrt(variance + EPSILON)
        normed = (hidden - spread(group_mean)) * spread(inv_spread)
        activated = (frame_mask * jax.nn.silu(normed * gain_row)).astype(jnp.bfloat16)
        padded_act = with_halo(activated, (("frame", 1),), 1)
        temporal = flat_dot(time_columns(padded_act, F_DEV), tkernel_flat).reshape(act_shape)
        output = (current.astype(jnp.float32) + temporal).astype(jnp.bfloat16)
        state = (padded_in, normed, padded_act, inv_spread)
        if kept is None:
            kept = state
        else:
            kept = tuple(jnp.where(is_live, new, old) for new, old in zip(state, kept))
        if tick == 0:
            skip = shifted(output, "segment", sections - 1)
        if tick < sections - 1:
            received = shifted(output, "segment", 1)
    padded_in, normed, padded_act, inv_spread = kept
    scaled = normed * gain_row
    gate_sig = jax.nn.sigmoid(scaled)
    slope = frame_mask * gate_sig * (1.0 + scaled * (1.0 - gate_sig))
    received = (frame_mask * cotangent.astype(jnp.float32)).astype(jnp.bfloat16)
    final = None
    for tick in range(sections):
        is_live = segment_index == sections - 1 - tick
        upstream = received
        if tick == sections - 1:
            upstream = (upstream.astype(jnp.float32) + skip.astype(jnp.float32)).astype(
                jnp.bfloat16
            )
        padded_up = with_halo(upstream, (("frame", 1),), 1)
        act_grad = flat_dot(time_flip(padded_up, F_DEV), tkernel_back).reshape(act_shape)
        scaled_grad = act_grad * slope
        normed_grad = scaled_grad * gain_row
        gathered = everyones(jnp.stack([group_sum(normed_grad), group_sum(normed_grad * normed)]))
        moments = jnp.sum(gathered, axis=0) / cell_total[None]
        hidden_grad = (
            spread(inv_spread)
            * (normed_grad - frame_mask * (spread(moments[0]) + normed * spread(moments[1])))
        ).astype(jnp.bfloat16)
        state = (upstream, scaled_grad, hidden_grad)
        if final is None:
            final = state
        else:
            final = tuple(jnp.where(is_live, new, old) for new, old in zip(state, final))
        if tick < sections - 1:
            padded_grad = with_halo(hidden_grad, (("row", 2),), 1)
            padded_grad = jnp.pad(padded_grad, ((0, 0), (0, 0), (0, 0), (1, 1), (0, 0)))
            conv_back = flat_dot(flip_columns(padded_grad, R_DEV, WIDTH), kernel_back).reshape(
                act_shape
            )
            input_grad = (upstream.astype(jnp.float32) + conv_back).astype(jnp.bfloat16)
            if tick == 0:
                skip = shifted(input_grad, "segment", -(sections - 1))
            received = shifted(input_grad, "segment", -1)
    upstream, scaled_grad, hidden_grad = final
    temporal_part = outer_dot(time_columns(padded_act, F_DEV), upstream)
    spatial_part = outer_dot(spatial_columns(padded_in, R_DEV, WIDTH), hidden_grad)
    gain_part = jnp.sum(scaled_grad * normed, axis=(0, 1, 2, 3))
    column_sums = jnp.sum(hidden_grad.astype(jnp.float32), axis=(1, 2, 3))
    rows_of = jnp.concatenate([column_sums, gain_part[None]], axis=0)
    totals = jnp.sum(everyones(rows_of), axis=0)
    spatial_out = scatter_sum(spatial_part)
    temporal_out = scatter_sum(temporal_part)
    place = lax.axis_index("frame") * lax.axis_size("row") + lax.axis_index("row")
    peers = lax.axis_size("frame") * lax.axis_size("row")
    gain_out = lax.dynamic_slice_in_dim(totals[CLIPS], place * (C // peers), C // peers)
    features = lax.dynamic_slice_in_dim(time_embed, place * (TE // peers), TE // peers, axis=1)
    features = features.astype(jnp.float32)
    time_out = sum(features[c][:, None] * totals[c][None, :] for c in range(CLIPS))
    return (spatial_out[None], temporal_out[None], time_out[None], gain_out[None])


def solution(mesh):
    return jax.shard_map(
        per_device,
        mesh=mesh,
        in_specs=(
            P(None, "frame", "row", None, None),
            P(None, "frame", "row", None, None),
            P(),
            P(),
            P("segment", None, None, None),
            P("segment", None, None, None),
            P("segment", None, None),
            P("segment", None),
        ),
        out_specs=(
            P("segment", ("frame", "row"), None),
            P("segment", ("frame", "row"), None),
            P("segment", ("frame", "row"), None),
            P("segment", ("frame", "row")),
        ),
        check_vma=False,
    )
```

```python
import functools

import jax
import jax.numpy as jnp
from jax import lax
from jax.experimental import pallas as pl
from jax.experimental.pallas import tpu as pltpu
from jax.sharding import PartitionSpec as P

C = 320
G = 32
TE = 1280
WIDTH = 24
PITCH = 32
ROWS = 8
R_DEV = 2
F_DEV = 2
CLIPS = 2
EPSILON = 1e-05

PLANE = ROWS * PITCH
CELLS = F_DEV * PLANE
UNIT = float(ROWS * WIDTH * (C // G))
PEERS = 16
VMEM_LIMIT = 20 * 1024 * 1024
F32 = jnp.float32
BF16 = jnp.bfloat16


def dot(a, b):
    return jnp.dot(a, b, preferred_element_type=F32)


def dot_back(a, b):
    return lax.dot_general(a, b, (((1,), (1,)), ((), ())), preferred_element_type=F32)


def exact_dot(a, b):
    return jnp.dot(a, b, preferred_element_type=F32, precision=lax.Precision.HIGHEST)


def to_groups():
    ch = lax.broadcasted_iota(jnp.int32, (C, 128), 0)
    low = lax.broadcasted_iota(jnp.int32, (C, 128), 1) * (C // G)
    return ((ch >= low) & (ch < low + C // G)).astype(F32)


def to_channels():
    ch = lax.broadcasted_iota(jnp.int32, (128, C), 1)
    low = lax.broadcasted_iota(jnp.int32, (128, C), 0) * (C // G)
    return ((ch >= low) & (ch < low + C // G)).astype(F32)


def col_mask(rows):
    at = lax.broadcasted_iota(jnp.int32, (rows, 1), 0)
    return (jnp.bitwise_and(at, PITCH - 1) < WIDTH).astype(F32)


def live_mask(first, limit, frames):
    parts = []
    for f in range(frames):
        ok = jnp.where((first + f >= 0) & (first + f < limit), 1.0, 0.0)
        parts.append(jnp.full((PLANE, 1), 1.0, F32) * ok)
    return jnp.concatenate(parts, axis=0) * col_mask(frames * PLANE)


def two_rows(top, second):
    return jnp.concatenate([top, second, jnp.zeros((6, top.shape[1]), F32)], axis=0)


def shifted_columns(x):
    rows = x.shape[0]
    gap = jnp.zeros((PITCH, 3 * C), BF16)
    wide = jnp.concatenate(
        [
            pltpu.roll(x, 1, 0).astype(BF16),
            x.astype(BF16),
            pltpu.roll(x, rows - 1, 0).astype(BF16),
        ],
        axis=1,
    )
    return jnp.concatenate([gap, wide[:PLANE], gap, wide[PLANE:], gap], axis=0)


SPAN = CELLS + PITCH


def without_gap(x):
    return jnp.concatenate([x[:PLANE], x[PLANE + PITCH :]], axis=0)


def conv(x, w_ref):
    wide = shifted_columns(x)
    total = None
    for a in range(3):
        taps = w_ref[3 * a : 3 * a + 3].reshape(3 * C, C)
        part = dot(wide[a * PITCH : a * PITCH + SPAN], taps)
        total = part if total is None else total + part
    return without_gap(total)


def conv_back(x, w_ref):
    wide = shifted_columns(x)
    total = None
    for a in range(3):
        taps = jnp.concatenate([w_ref[3 * a + 2], w_ref[3 * a + 1], w_ref[3 * a]], axis=1)
        part = dot_back(wide[(2 - a) * PITCH : (2 - a) * PITCH + SPAN], taps)
        total = part if total is None else total + part
    return without_gap(total)


def joined_stats(gathered_ref, limit):
    means = gathered_ref[:, 0, :]
    squares = gathered_ref[:, 1, :]
    peer = lax.broadcasted_iota(jnp.int32, (PEERS, 128), 0)
    held = jnp.clip(limit - peer * F_DEV, 0, F_DEV).astype(F32) * UNIT
    total = limit.astype(F32) * UNIT
    mean = jnp.sum(held * means, axis=0, keepdims=True) / total
    apart = means - mean
    variance = jnp.sum(squares + held * apart * apart, axis=0, keepdims=True) / total
    both = exact_dot(two_rows(mean, lax.rsqrt(variance + EPSILON)), to_channels())
    sums = from_lanes(jnp.sum(gathered_ref[...], axis=0), 2) * both[1:2]
    return jnp.concatenate([both[0:2], sums, jnp.zeros((5, C), F32)], axis=0)


def in_lanes(row):
    tail = jnp.concatenate([row[:, 256:], jnp.zeros((1, 3 * 128 - C), F32)], axis=1)
    return [row[:, :128], row[:, 128:256], tail]


def from_lanes(sums, at):
    parts = [sums[at : at + 1], sums[at + 1 : at + 2], sums[at + 2 : at + 3, : C - 256]]
    return jnp.concatenate(parts, axis=1)


def own_stats(hidden, mask, first, limit):
    held = jnp.clip(limit - first, 0, F_DEV).astype(F32) * UNIT
    sums = jnp.sum(hidden * mask, axis=0, keepdims=True)
    pad = jnp.zeros_like(sums)
    mean = exact_dot(two_rows(sums, pad), to_groups()) / jnp.maximum(held, 1.0)
    off = hidden - exact_dot(mean, to_channels())[0:1]
    square = jnp.sum(off * off * mask, axis=0, keepdims=True)
    square = exact_dot(two_rows(pad, square), to_groups())
    by_channel = jnp.sum(off * mask, axis=0, keepdims=True)
    rest = [jnp.zeros((3, 128), F32)]
    return jnp.concatenate([mean[0:1], square[1:2]] + in_lanes(by_channel) + rest, axis=0)


def put_stats(stats, out_ref):
    for peer in range(PEERS):
        out_ref[peer] = stats


def conv_kernel(place, x_ref, w_ref, bias_ref, hidden_ref, stats_ref):
    hidden = conv(x_ref[...].astype(F32), w_ref) + bias_ref[...]
    hidden_ref[...] = hidden
    first, limit = place[0], place[1]
    put_stats(own_stats(hidden, live_mask(first, limit, F_DEV), first, limit), stats_ref)


def activate(place, hidden, moments, gain, frames_before, frames):
    normed = (hidden - moments[0:1]) * moments[1:2]
    scaled = normed * gain
    mask = live_mask(place[0] - frames_before, place[1], frames)
    return (mask * (scaled * jax.nn.sigmoid(scaled))).astype(BF16)


def activate_all(place, before_ref, hidden_ref, after_ref, gathered_ref, gain_ref, act_ref, moments_ref):
    moments = joined_stats(gathered_ref, place[1])
    moments_ref[...] = moments
    gain = gain_ref[...]
    act_ref[:PLANE] = activate(place, before_ref[...], moments, gain, 1, 1)
    act_ref[PLANE : PLANE + CELLS] = activate(place, hidden_ref[...], moments, gain, 0, F_DEV)
    act_ref[PLANE + CELLS :] = activate(place, after_ref[...], moments, gain, -F_DEV, 1)


def section_output(act_ref, x_ref, t_ref):
    wide = jnp.concatenate([act_ref[k * PLANE : k * PLANE + CELLS] for k in range(3)], axis=1)
    temporal = dot(wide, t_ref[...].reshape(3 * C, C))
    return (x_ref[...].astype(F32) + temporal).astype(BF16)


def output_kernel(
    place, before, hidden, after, gathered, gain, x, t, act_ref, moments_ref, out_ref
):
    activate_all(place, before, hidden, after, gathered, gain, act_ref, moments_ref)
    out_ref[...] = section_output(act_ref, x, t)


def section_kernel(joins, place, before, hidden, after, gathered, gain, x, t, *rest):
    if joins:
        skip, w, bias, act_ref, moments_ref, out_ref, hidden_ref, stats_ref = rest
    else:
        w, bias, act_ref, moments_ref, out_ref, hidden_ref, stats_ref = rest
    activate_all(place, before, hidden, after, gathered, gain, act_ref, moments_ref)
    out = section_output(act_ref, x, t)
    if joins:
        out = (out.astype(F32) + skip[...].astype(F32)).astype(BF16)
    out_ref[...] = out
    conv_kernel(place, out_ref, w, bias, hidden_ref, stats_ref)


def act_grad_kernel(
    mode, place, u_before, u, u_after, *rest
):
    first, limit = place[0], place[1]
    if mode == "last":
        (before, hidden, after, gathered, gain_ref, t, act_ref, moments_ref, grad_ref, sums_ref) = rest
        activate_all(place, before, hidden, after, gathered, gain_ref, act_ref, moments_ref)
        planes = [u_before[...], u[...], u_after[...]]
    elif mode == "first":
        (s_before, s, s_after, hidden, moments_ref, gain_ref, t, u_out, grad_ref, sums_ref) = rest
        planes = [
            (p[...].astype(F32) + q[...].astype(F32)).astype(BF16)
            for p, q in ((u_before, s_before), (u, s), (u_after, s_after))
        ]
        u_out[...] = planes[1]
    else:
        hidden, moments_ref, gain_ref, t, grad_ref, sums_ref = rest
        planes = [u_before[...], u[...], u_after[...]]
    ext = jnp.concatenate(planes, axis=0)
    wide = jnp.concatenate([ext[(2 - k) * PLANE : (2 - k) * PLANE + CELLS] for k in range(3)], axis=1)
    taps = jnp.concatenate([t[0], t[1], t[2]], axis=1)
    act_grad = dot_back(wide, taps)
    gain = gain_ref[...]
    normed = (hidden[...] - moments_ref[0:1]) * moments_ref[1:2]
    scaled = normed * gain
    gate = jax.nn.sigmoid(scaled)
    scaled_grad = act_grad * live_mask(first, limit, F_DEV) * gate * (1.0 + scaled * (1.0 - gate))
    by_normed = jnp.sum(scaled_grad * normed, axis=0, keepdims=True)
    grad = scaled_grad * gain
    grad_ref[...] = grad
    plain = jnp.sum(grad, axis=0, keepdims=True)
    groups = exact_dot(two_rows(plain, by_normed * gain), to_groups())
    rows = [groups[0:2]] + in_lanes(plain) + in_lanes(by_normed)
    put_stats(jnp.concatenate(rows, axis=0), sums_ref)


def hidden_grad(place, grad_ref, hidden_ref, moments_ref, sums_ref, hg_ref, col_ref):
    first, limit = place[0], place[1]
    total = limit.astype(F32) * UNIT
    sums = jnp.sum(sums_ref[...], axis=0)
    means = exact_dot(sums, to_channels()) / total
    normed = (hidden_ref[...] - moments_ref[0:1]) * moments_ref[1:2]
    mask = live_mask(first, limit, F_DEV)
    hg = moments_ref[1:2] * (grad_ref[...] - mask * (means[0:1] + normed * means[1:2]))
    hg = hg.astype(BF16)
    hg_ref[...] = hg
    cells = limit.astype(F32) * (ROWS * WIDTH)
    col = from_lanes(sums, 2) - means[0:1] * cells - means[1:2] * moments_ref[2:3]
    col_ref[...] = two_rows(moments_ref[1:2] * col, from_lanes(sums, 5))
    return hg.astype(F32)


def input_grad_kernel(place, grad, hidden, moments, sums, u, w, hg_ref, col_ref, out_ref):
    hg = hidden_grad(place, grad, hidden, moments, sums, hg_ref, col_ref)
    out = u[...].astype(F32) + conv_back(hg, w)
    out_ref[...] = (out * col_mask(CELLS)).astype(BF16)


def hidden_grad_kernel(place, grad, hidden, moments, sums, hg_ref, col_ref):
    hidden_grad(place, grad, hidden, moments, sums, hg_ref, col_ref)


ACT = ((CELLS, C), BF16)
HID = ((CELLS, C), F32)
EXT = (((F_DEV + 2) * PLANE, C), BF16)
ROW8 = ((8, C), F32)
STATS = ((PEERS, 8, 128), F32)


def run(kernel, place, args, outs, name):
    vmem = pl.BlockSpec(memory_space=pltpu.VMEM)
    return pl.pallas_call(
        kernel,
        out_shape=tuple(jax.ShapeDtypeStruct(s, d) for s, d in outs),
        in_specs=[pl.BlockSpec(memory_space=pltpu.SMEM)] + [vmem] * len(args),
        out_specs=tuple(vmem for _ in outs),
        name=name,
        compiler_params=pltpu.CompilerParams(vmem_limit_bytes=VMEM_LIMIT),
    )(place, *args)


def assemble_kernel(place, w, t, *rest):
    got, (w_out, t_out, sems) = rest[:8], rest[8:]
    back, core = place[2], place[3]

    def pieces(lower, upper):
        targets = (w_out.at[pl.ds(0, 3)], w_out.at[pl.ds(3, 3)], w_out.at[pl.ds(6, 3)], t_out)
        return [
            pltpu.make_async_copy(ref, target, sems.at[n])
            for n, (ref, target) in enumerate(zip(lower + upper, targets))
        ]

    def both(ref):
        return [ref.at[pl.ds(0, 3)], ref.at[pl.ds(3, 3)]]

    def go(jobs):
        for job in jobs:
            job.start()
        for job in jobs:
            job.wait()

    @pl.when(back == 0)
    def _():
        go([
            pltpu.make_async_copy(w, w_out, sems.at[0]),
            pltpu.make_async_copy(t, t_out, sems.at[1]),
        ])

    near, near_other, far, far_other, on_a, on_a_other, on_b, on_b_other = got
    held = {
        1: (both(near), both(near_other)),
        2: ([on_a, on_b], [on_a_other, on_b_other]),
        3: (both(far), both(far_other)),
    }
    for d, (mine, other) in held.items():
        for c in range(2):

            @pl.when((back == d) & (core == c))
            def _(mine=mine, other=other, c=c):
                go(pieces(mine, other) if c == 0 else pieces(other, mine))


def assemble(place, w, t, got):
    anywhere = pl.BlockSpec(memory_space=pl.ANY)
    vmem = pl.BlockSpec(memory_space=pltpu.VMEM)
    return pl.pallas_call(
        assemble_kernel,
        out_shape=(
            jax.ShapeDtypeStruct((9, C, C), BF16),
            jax.ShapeDtypeStruct((3, C, C), BF16),
        ),
        in_specs=[pl.BlockSpec(memory_space=pltpu.SMEM)] + [anywhere] * 10,
        out_specs=(vmem, vmem),
        scratch_shapes=[pltpu.SemaphoreType.DMA((4,))],
        name="assemble",
    )(place, w, t, *got)


def weight_grad_kernel(place, *refs):
    lists, (keep_ref, give_ref), scratch = refs[:16], refs[16:18], refs[18:]
    bufs, spatial, temporal, chunks, sems = scratch[:4], *scratch[4:]
    segment, core, half = place[0], place[1], place[2]
    for k in range(4):

        @pl.when(segment == k)
        def _(k=k):
            jobs = [
                pltpu.make_async_copy(lists[4 * k + n], bufs[n], sems.at[n]) for n in range(4)
            ]
            for job in jobs:
                job.start()
            for job in jobs:
                job.wait()

    x, hg, act, u = bufs
    wide = shifted_columns(x[...].astype(F32))
    hidden_grad = hg[...]
    gap = jnp.zeros((PITCH, C), BF16)
    spread_grad = jnp.concatenate([hidden_grad[:PLANE], gap, hidden_grad[PLANE:]], axis=0)
    over_cells = (((0,), (0,)), ((), ()))
    for a in range(3):
        spatial[3 * C * a : 3 * C * (a + 1)] = lax.dot_general(
            wide[a * PITCH : a * PITCH + SPAN], spread_grad, over_cells, preferred_element_type=F32
        )
    upstream = u[...]
    for k in range(3):
        temporal[C * k : C * (k + 1)] = lax.dot_general(
            act[k * PLANE : k * PLANE + CELLS], upstream, over_cells, preferred_element_type=F32
        )
    for n in range(2 * PEERS):
        both = jnp.concatenate([spatial[90 * n : 90 * n + 90], temporal[30 * n : 30 * n + 30]], axis=0)
        chunks[n] = both.astype(BF16)
    for q in range(PEERS // 2):
        keep_ref[q] = chunks[4 * q + 2 * core + half]
        give_ref[q] = chunks[4 * q + 2 * (1 - core) + half]


def weight_grads(place, kept):
    anywhere = pl.BlockSpec(memory_space=pl.ANY)
    vmem = pl.BlockSpec(memory_space=pltpu.VMEM)
    lists = [state[name] for state in kept for name in ("x", "hg", "act", "u")]
    chunk = jax.ShapeDtypeStruct((PEERS // 2, 120, C), BF16)
    return pl.pallas_call(
        weight_grad_kernel,
        out_shape=(chunk, chunk),
        in_specs=[pl.BlockSpec(memory_space=pltpu.SMEM)] + [anywhere] * 16,
        out_specs=(vmem, vmem),
        scratch_shapes=[
            pltpu.VMEM((CELLS, C), BF16),
            pltpu.VMEM((CELLS, C), BF16),
            pltpu.VMEM(((F_DEV + 2) * PLANE, C), BF16),
            pltpu.VMEM((CELLS, C), BF16),
            pltpu.VMEM((9 * C, C), F32),
            pltpu.VMEM((3 * C, C), F32),
            pltpu.VMEM((2 * PEERS, 120, C), BF16),
            pltpu.SemaphoreType.DMA((4,)),
        ],
        name="weight_grads",
        compiler_params=pltpu.CompilerParams(vmem_limit_bytes=VMEM_LIMIT),
    )(place, *lists)


def time_features(timesteps):
    half_dim = TE // 2
    frequency = jnp.exp(-jnp.log(10000.0) * jnp.arange(half_dim).astype(jnp.float32) / half_dim)
    angles = timesteps.astype(jnp.float32)[:, None] * frequency[None, :]
    wave_parts = jnp.concatenate([jnp.cos(angles), jnp.sin(angles)], axis=1)
    return jax.nn.silu(wave_parts).astype(jnp.bfloat16)


def whole_frames(array):
    rows = lax.axis_size("row")
    split = array[jnp.arange(rows) % CLIPS]
    got = lax.all_to_all(split, "row", 0, 0)
    got = jnp.transpose(got, (1, 0, 2, 3, 4)).reshape(F_DEV, ROWS, WIDTH, C)
    return jnp.pad(got, ((0, 0), (0, 0), (0, PITCH - WIDTH), (0, 0))).reshape(CELLS, C)


def exchange(stats):
    return lax.all_to_all(stats, "frame", 0, 0)


def halo(array):
    up = [(i, i + 1) for i in range(PEERS - 1)]
    before = lax.ppermute(array[CELLS - PLANE :], "frame", up)
    after = lax.ppermute(array[:PLANE], "frame", [(j, i) for i, j in up])
    return before, after


def from_segment_zero(array, segment_index, sections):
    got = [lax.ppermute(array, "segment", [(0, j)]) for j in range(1, sections)]
    return jnp.where(segment_index == 0, array, sum(got[1:], got[0]))


def pick(options, segment_index):
    out = options[0]
    for k in range(1, len(options)):
        out = jnp.where(segment_index == k, options[k], out)
    return out


def per_device(
    latents,
    cotangent,
    timesteps,
    frame_counts,
    spatial_weight,
    temporal_weight,
    time_weight,
    norm_gain,
):
    sections = lax.axis_size("segment")
    segment_index = lax.axis_index("segment")
    frame_index = lax.axis_index("frame")
    row_index = lax.axis_index("row")
    clip = row_index % CLIPS
    core = frame_index % 2
    kernel = spatial_weight[0]
    tkernel = temporal_weight[0]

    limit = lax.dynamic_index_in_dim(frame_counts, clip, 0, keepdims=False)
    first = frame_index * F_DEV

    def place_of(k):
        back = (segment_index - k) % sections
        return jnp.stack([first, limit, back, core]).astype(jnp.int32)

    place = place_of(0)

    half = jnp.where(core == 0, kernel[:6], jnp.concatenate([kernel[6:], tkernel], axis=0))
    time_embed = time_features(timesteps)
    biases = jnp.dot(time_embed, time_weight[0], preferred_element_type=jnp.float32)
    own_rows = jnp.concatenate([biases, norm_gain, jnp.zeros((5, C), F32)], axis=0)
    x = whole_frames(latents)
    rows_from = [own_rows]
    for d in range(1, sections):
        pairs = [(k, (k + d) % sections) for k in range(sections)]
        rows_from.append(lax.ppermute(own_rows, "segment", pairs))
    swap = [(i, i ^ 1) for i in range(PEERS)]
    near = lax.ppermute(half, "segment", [(1, 2), (2, 3), (3, 0)])
    far = lax.ppermute(half, "segment", [(1, 0), (2, 1), (3, 2)])

    def rows_of(k):
        rows = pick(rows_from, (segment_index - k) % sections)
        bias = jnp.where(clip == 0, rows[0:1], rows[1:2])
        return bias, rows[2:3]

    own_bias = jnp.where(clip == 0, biases[0:1], biases[1:2])
    cot = whole_frames(cotangent)
    ids = first + jnp.arange(F_DEV)
    used = jnp.repeat(ids < limit, PLANE)[:, None]
    cot = jnp.where(used, cot, jnp.zeros_like(cot))
    cot_before, cot_after = halo(cot)

    hidden, stats = run(conv_kernel, place, (x, kernel, own_bias), (HID, STATS), "conv0")
    before, after = halo(hidden)
    gathered = exchange(stats)
    gathered, near, far, *rows_from = lax.optimization_barrier((gathered, near, far, *rows_from))
    on_a = lax.ppermute(near[:3], "segment", [(2, 3), (3, 0), (0, 1)])
    on_b = lax.ppermute(far[3:], "segment", [(0, 3), (1, 0), (2, 1)])
    near_other = lax.ppermute(near, "frame", swap)
    far_other = lax.ppermute(far, "frame", swap)
    act, moments, out = run(
        output_kernel,
        place,
        (before, hidden, after, gathered, norm_gain, x, tkernel),
        (EXT, ROW8, ACT),
        "output0",
    )
    kept = [dict(x=x, hidden=hidden, act=act, moments=moments)]
    x = from_segment_zero(out, segment_index, sections)
    x, on_a, on_b = lax.optimization_barrier((x, on_a, on_b))
    on_a_other = lax.ppermute(on_a, "frame", swap)
    on_b_other = lax.ppermute(on_b, "frame", swap)
    fetched = (near, near_other, far, far_other, on_a, on_a_other, on_b, on_b_other)
    skip = x
    weights = [(kernel, tkernel)]
    gains = [norm_gain]
    for k in range(1, sections):
        weights.append(assemble(place_of(k), kernel, tkernel, fetched))
        bias, gain = rows_of(k)
        gains.append(gain)
        if k == 1:
            hidden, stats = run(
                conv_kernel, place, (x, weights[k][0], bias), (HID, STATS), "conv1"
            )
        else:
            joins = k == sections - 1
            args = (before, hidden, after, gathered, gains[k - 1], x, weights[k - 1][1])
            args += (skip,) if joins else ()
            act, moments, x, hidden, stats = run(
                functools.partial(section_kernel, joins),
                place,
                args + (weights[k][0], bias),
                (EXT, ROW8, ACT, HID, STATS),
                f"section{k}",
            )
            kept[k - 1].update(act=act, moments=moments)
        kept.append(dict(x=x, hidden=hidden))
        before, after = halo(hidden)
        gathered = exchange(stats)

    u, u_before, u_after = cot, cot_before, cot_after
    skip_u = None
    for k in reversed(range(sections)):
        state = kept[k]
        sides = (u_before, u, u_after)
        if k == sections - 1:
            act, moments, grad, sums = run(
                functools.partial(act_grad_kernel, "last"),
                place,
                sides + (before, state["hidden"], after, gathered, gains[k], weights[k][1]),
                (EXT, ROW8, HID, STATS),
                "act_grad_last",
            )
            state.update(act=act, moments=moments)
        elif k == 0:
            u, grad, sums = run(
                functools.partial(act_grad_kernel, "first"),
                place,
                sides + skip_u + (state["hidden"], state["moments"], gains[k], weights[k][1]),
                (ACT, HID, STATS),
                "act_grad_first",
            )
        else:
            grad, sums = run(
                functools.partial(act_grad_kernel, "mid"),
                place,
                sides + (state["hidden"], state["moments"], gains[k], weights[k][1]),
                (HID, STATS),
                f"act_grad{k}",
            )
        state.update(u=u)
        sums = exchange(sums)
        args = (grad, state["hidden"], state["moments"], sums)
        if k > 0:
            hg, col, u = run(
                input_grad_kernel, place, args + (u, weights[k][0]), (ACT, ROW8, ACT), f"input_grad{k}"
            )
            u_before, u_after = halo(u)
            if k == sections - 1:
                skip_u = (u_before, u, u_after)
        else:
            hg, col = run(hidden_grad_kernel, place, args, (ACT, ROW8), "hidden_grad0")
        state.update(hg=hg, col=col)

    pair, side = row_index // 2, row_index % 2
    partner = [(i, i ^ 1) for i in range(4)]
    keep, give = weight_grads(jnp.stack([segment_index, core, pair]).astype(jnp.int32), kept)
    got = lax.ppermute(give, "frame", swap)
    col = pick([state["col"] for state in kept], segment_index)
    other = lax.ppermute(col, "row", partner)
    summed = (keep.astype(F32) + got.astype(F32)).astype(BF16)
    groups = [[i for i in range(PEERS) if i % 2 == c] for c in range(2)]
    summed = lax.all_to_all(summed, "frame", 0, 0, axis_index_groups=groups)
    summed = jnp.sum(summed.astype(F32), axis=0)
    spatial_rows, temporal_rows = 9 * C // (4 * PEERS), 3 * C // (4 * PEERS)

    def part(of):
        spatial = lax.dynamic_slice_in_dim(summed[:90], of * spatial_rows, spatial_rows)
        temporal = lax.dynamic_slice_in_dim(summed[90:], of * temporal_rows, temporal_rows)
        return jnp.concatenate([spatial, temporal], axis=0)

    summed = part(side) + lax.ppermute(part(1 - side), "row", partner)
    spatial_out, temporal_out = summed[:spatial_rows], summed[spatial_rows:]

    peers = 4 * PEERS
    gain_total = col[1] + other[1]
    totals = [jnp.where(clip == c, col[0], other[0]) for c in range(CLIPS)]
    spot = frame_index * 4 + row_index
    gain_out = lax.dynamic_slice_in_dim(gain_total, spot * (C // peers), C // peers)
    features = lax.dynamic_slice_in_dim(time_embed, spot * (TE // peers), TE // peers, axis=1)
    features = features.astype(F32)
    time_out = sum(features[c][:, None] * totals[c][None, :] for c in range(CLIPS))
    return (spatial_out[None], temporal_out[None], time_out[None], gain_out[None])


def solution(mesh):
    return jax.shard_map(
        per_device,
        mesh=mesh,
        in_specs=(
            P(None, "frame", "row", None, None),
            P(None, "frame", "row", None, None),
            P(),
            P(),
            P("segment", None, None, None),
            P("segment", None, None, None),
            P("segment", None, None),
            P("segment", None),
        ),
        out_specs=(
            P("segment", ("frame", "row"), None),
            P("segment", ("frame", "row"), None),
            P("segment", ("frame", "row"), None),
            P("segment", ("frame", "row")),
        ),
        check_vma=False,
    )
```

```python
import functools

import jax
import jax.numpy as jnp
from jax import lax
from jax.experimental import pallas as pl
from jax.experimental.pallas import tpu as pltpu
from jax.sharding import PartitionSpec as P

C = 320
G = 32
TE = 1280
WIDTH = 24
PITCH = 32
ROWS = 8
R_DEV = 2
F_DEV = 2
CLIPS = 2
EPSILON = 1e-05

PLANE = ROWS * PITCH
CELLS = F_DEV * PLANE
UNIT = float(ROWS * WIDTH * (C // G))
PEERS = 16
PADDED = 384
VMEM_LIMIT = 20 * 1024 * 1024
F32 = jnp.float32
BF16 = jnp.bfloat16


def dot(a, b):
    return jnp.dot(a, b, preferred_element_type=F32)


def dot_back(a, b):
    return lax.dot_general(a, b, (((1,), (1,)), ((), ())), preferred_element_type=F32)


def exact_dot(a, b):
    return jnp.dot(a, b, preferred_element_type=F32, precision=lax.Precision.HIGHEST)


def to_groups():
    ch = lax.broadcasted_iota(jnp.int32, (C, 128), 0)
    low = lax.broadcasted_iota(jnp.int32, (C, 128), 1) * (C // G)
    return ((ch >= low) & (ch < low + C // G)).astype(F32)


def to_channels():
    ch = lax.broadcasted_iota(jnp.int32, (128, C), 1)
    low = lax.broadcasted_iota(jnp.int32, (128, C), 0) * (C // G)
    return ((ch >= low) & (ch < low + C // G)).astype(F32)


def col_mask(rows):
    at = lax.broadcasted_iota(jnp.int32, (rows, 1), 0)
    return (jnp.bitwise_and(at, PITCH - 1) < WIDTH).astype(F32)


def live_mask(first, limit, frames):
    parts = []
    for f in range(frames):
        ok = jnp.where((first + f >= 0) & (first + f < limit), 1.0, 0.0)
        parts.append(jnp.full((PLANE, 1), 1.0, F32) * ok)
    return jnp.concatenate(parts, axis=0) * col_mask(frames * PLANE)


def two_rows(top, second):
    return jnp.concatenate([top, second, jnp.zeros((6, top.shape[1]), F32)], axis=0)


def shifted_columns(x):
    rows = x.shape[0]
    gap = jnp.zeros((PITCH, 3 * C), BF16)
    wide = jnp.concatenate(
        [
            pltpu.roll(x, 1, 0).astype(BF16),
            x.astype(BF16),
            pltpu.roll(x, rows - 1, 0).astype(BF16),
        ],
        axis=1,
    )
    return jnp.concatenate([gap, wide[:PLANE], gap, wide[PLANE:], gap], axis=0)


SPAN = CELLS + PITCH


def without_gap(x):
    return jnp.concatenate([x[:PLANE], x[PLANE + PITCH :]], axis=0)


def conv(x, w_ref):
    wide = shifted_columns(x)
    total = None
    for a in range(3):
        taps = w_ref[3 * a : 3 * a + 3].reshape(3 * C, C)
        part = dot(wide[a * PITCH : a * PITCH + SPAN], taps)
        total = part if total is None else total + part
    return without_gap(total)


def conv_back(x, w_ref):
    wide = shifted_columns(x)
    total = None
    for a in range(3):
        taps = jnp.concatenate([w_ref[3 * a + 2], w_ref[3 * a + 1], w_ref[3 * a]], axis=1)
        part = dot_back(wide[(2 - a) * PITCH : (2 - a) * PITCH + SPAN], taps)
        total = part if total is None else total + part
    return without_gap(total)


def joined_stats(gathered_ref, limit):
    means = gathered_ref[:, 0, :]
    squares = gathered_ref[:, 1, :]
    peer = lax.broadcasted_iota(jnp.int32, (PEERS, 128), 0)
    held = jnp.clip(limit - peer * F_DEV, 0, F_DEV).astype(F32) * UNIT
    total = limit.astype(F32) * UNIT
    mean = jnp.sum(held * means, axis=0, keepdims=True) / total
    apart = means - mean
    variance = jnp.sum(squares + held * apart * apart, axis=0, keepdims=True) / total
    both = exact_dot(two_rows(mean, lax.rsqrt(variance + EPSILON)), to_channels())
    sums = from_lanes(jnp.sum(gathered_ref[...], axis=0), 2) * both[1:2]
    return jnp.concatenate([both[0:2], sums, jnp.zeros((5, C), F32)], axis=0)


def in_lanes(row):
    tail = jnp.concatenate([row[:, 256:], jnp.zeros((1, 3 * 128 - C), F32)], axis=1)
    return [row[:, :128], row[:, 128:256], tail]


def from_lanes(sums, at):
    parts = [sums[at : at + 1], sums[at + 1 : at + 2], sums[at + 2 : at + 3, : C - 256]]
    return jnp.concatenate(parts, axis=1)


def own_stats(hidden, mask, first, limit):
    held = jnp.clip(limit - first, 0, F_DEV).astype(F32) * UNIT
    sums = jnp.sum(hidden * mask, axis=0, keepdims=True)
    pad = jnp.zeros_like(sums)
    mean = exact_dot(two_rows(sums, pad), to_groups()) / jnp.maximum(held, 1.0)
    off = hidden - exact_dot(mean, to_channels())[0:1]
    square = jnp.sum(off * off * mask, axis=0, keepdims=True)
    square = exact_dot(two_rows(pad, square), to_groups())
    by_channel = jnp.sum(off * mask, axis=0, keepdims=True)
    rest = [jnp.zeros((3, 128), F32)]
    return jnp.concatenate([mean[0:1], square[1:2]] + in_lanes(by_channel) + rest, axis=0)


def put_stats(stats, out_ref):
    for peer in range(PEERS):
        out_ref[peer] = stats


def put_edges(value, low_ref, high_ref):
    low_ref[...] = value[:PLANE]
    high_ref[...] = value[CELLS - PLANE :]


def conv_kernel(place, x_ref, w_ref, bias_ref, hidden_ref, low_ref, high_ref, stats_ref):
    hidden = conv(x_ref[...].astype(F32), w_ref) + bias_ref[...]
    hidden_ref[...] = hidden
    put_edges(hidden, low_ref, high_ref)
    first, limit = place[0], place[1]
    put_stats(own_stats(hidden, live_mask(first, limit, F_DEV), first, limit), stats_ref)


def activate(place, hidden, moments, gain, frames_before, frames):
    normed = (hidden - moments[0:1]) * moments[1:2]
    scaled = normed * gain
    mask = live_mask(place[0] - frames_before, place[1], frames)
    return (mask * (scaled * jax.nn.sigmoid(scaled))).astype(BF16)


def activate_all(place, before_ref, hidden_ref, after_ref, gathered_ref, gain_ref, act_ref, moments_ref):
    moments = joined_stats(gathered_ref, place[1])
    moments_ref[...] = moments
    gain = gain_ref[...]
    act_ref[:PLANE] = activate(place, before_ref[...], moments, gain, 1, 1)
    act_ref[PLANE : PLANE + CELLS] = activate(place, hidden_ref[...], moments, gain, 0, F_DEV)
    act_ref[PLANE + CELLS :] = activate(place, after_ref[...], moments, gain, -F_DEV, 1)


def section_output(act_ref, x_ref, t_ref):
    wide = jnp.concatenate([act_ref[k * PLANE : k * PLANE + CELLS] for k in range(3)], axis=1)
    temporal = dot(wide, t_ref[...].reshape(3 * C, C))
    return (x_ref[...].astype(F32) + temporal).astype(BF16)


def output_kernel(
    place, before, hidden, after, gathered, gain, x, t, act_ref, moments_ref, out_ref
):
    activate_all(place, before, hidden, after, gathered, gain, act_ref, moments_ref)
    out_ref[...] = section_output(act_ref, x, t)


def fetch(place, sources, w_out, t_out, sems, begin):
    w, t, near, near_other, far, far_other, on, on_other = sources
    back, core = place[2], place[3]

    def go(*pairs):
        for n, (source, target) in enumerate(pairs):
            job = pltpu.make_async_copy(source, target, sems.at[n])
            if begin:
                job.start()
            else:
                job.wait()

    @pl.when(back == 0)
    def _():
        go((w, w_out), (t, t_out))

    for d, held in ((1, (near, near_other)), (2, (on, on_other)), (3, (far, far_other))):
        for c in range(2):

            @pl.when((back == d) & (core == c))
            def _(lower=held[c], upper=held[1 - c]):
                go(
                    (lower, w_out.at[pl.ds(0, 6)]),
                    (upper.at[pl.ds(0, 3)], w_out.at[pl.ds(6, 3)]),
                    (upper.at[pl.ds(3, 3)], t_out),
                )


def fetched_conv_kernel(place, x, bias, *rest):
    sources, (hidden_ref, low, high, stats, w_out, t_out), sems = rest[:8], rest[8:14], rest[14]
    fetch(place, sources, w_out, t_out, sems, True)
    fetch(place, sources, w_out, t_out, sems, False)
    conv_kernel(place, x, w_out, bias, hidden_ref, low, high, stats)


def section_kernel(joins, place, before, hidden, after, gathered, gain, x, t, bias, *rest):
    if joins:
        skip, rest = rest[0], rest[1:]
    sources, rest = rest[:8], rest[8:]
    act_ref, moments_ref, out_ref, hidden_ref, low, high, stats_ref, w_out, t_out, sems = rest
    fetch(place, sources, w_out, t_out, sems, True)
    activate_all(place, before, hidden, after, gathered, gain, act_ref, moments_ref)
    out = section_output(act_ref, x, t)
    if joins:
        out = (out.astype(F32) + skip[...].astype(F32)).astype(BF16)
    out_ref[...] = out
    fetch(place, sources, w_out, t_out, sems, False)
    conv_kernel(place, out_ref, w_out, bias, hidden_ref, low, high, stats_ref)


def act_grad_kernel(
    mode, place, u_before, u, u_after, *rest
):
    first, limit = place[0], place[1]
    if mode == "last":
        (before, hidden, after, gathered, gain_ref, t, act_ref, moments_ref, grad_ref, sums_ref) = rest
        activate_all(place, before, hidden, after, gathered, gain_ref, act_ref, moments_ref)
        planes = [u_before[...], u[...], u_after[...]]
    elif mode == "first":
        (s_before, s, s_after, hidden, moments_ref, gain_ref, t, u_out, grad_ref, sums_ref) = rest
        planes = [
            (p[...].astype(F32) + q[...].astype(F32)).astype(BF16)
            for p, q in ((u_before, s_before), (u, s), (u_after, s_after))
        ]
        u_out[...] = planes[1]
    else:
        hidden, moments_ref, gain_ref, t, grad_ref, sums_ref = rest
        planes = [u_before[...], u[...], u_after[...]]
    ext = jnp.concatenate(planes, axis=0)
    wide = jnp.concatenate([ext[(2 - k) * PLANE : (2 - k) * PLANE + CELLS] for k in range(3)], axis=1)
    taps = jnp.concatenate([t[0], t[1], t[2]], axis=1)
    act_grad = dot_back(wide, taps)
    gain = gain_ref[...]
    normed = (hidden[...] - moments_ref[0:1]) * moments_ref[1:2]
    scaled = normed * gain
    gate = jax.nn.sigmoid(scaled)
    scaled_grad = act_grad * live_mask(first, limit, F_DEV) * gate * (1.0 + scaled * (1.0 - gate))
    by_normed = jnp.sum(scaled_grad * normed, axis=0, keepdims=True)
    grad = scaled_grad * gain
    grad_ref[...] = grad
    plain = jnp.sum(grad, axis=0, keepdims=True)
    groups = exact_dot(two_rows(plain, by_normed * gain), to_groups())
    rows = [groups[0:2]] + in_lanes(plain) + in_lanes(by_normed)
    put_stats(jnp.concatenate(rows, axis=0), sums_ref)


def hidden_grad(place, grad_ref, hidden_ref, moments_ref, sums_ref, hg_ref, col_ref):
    first, limit = place[0], place[1]
    total = limit.astype(F32) * UNIT
    sums = jnp.sum(sums_ref[...], axis=0)
    means = exact_dot(sums, to_channels()) / total
    normed = (hidden_ref[...] - moments_ref[0:1]) * moments_ref[1:2]
    mask = live_mask(first, limit, F_DEV)
    hg = moments_ref[1:2] * (grad_ref[...] - mask * (means[0:1] + normed * means[1:2]))
    hg = hg.astype(BF16)
    hg_ref[...] = hg
    cells = limit.astype(F32) * (ROWS * WIDTH)
    col = from_lanes(sums, 2) - means[0:1] * cells - means[1:2] * moments_ref[2:3]
    col_ref[...] = two_rows(moments_ref[1:2] * col, from_lanes(sums, 5))
    return hg.astype(F32)


def input_grad_kernel(place, grad, hidden, moments, sums, u, w, hg_ref, col_ref, out_ref, low, high):
    hg = hidden_grad(place, grad, hidden, moments, sums, hg_ref, col_ref)
    out = u[...].astype(F32) + conv_back(hg, w)
    out = (out * col_mask(CELLS)).astype(BF16)
    out_ref[...] = out
    put_edges(out, low, high)


def hidden_grad_kernel(place, grad, hidden, moments, sums, hg_ref, col_ref):
    hidden_grad(place, grad, hidden, moments, sums, hg_ref, col_ref)


ACT = ((CELLS, C), BF16)
HID = ((CELLS, C), F32)
EXT = (((F_DEV + 2) * PLANE, C), BF16)
ROW8 = ((8, C), F32)
STATS = ((PEERS, 8, 128), F32)


EDGE = ((PLANE, C), BF16)
WIDE_EDGE = ((PLANE, C), F32)
CONV_OUT = (HID, WIDE_EDGE, WIDE_EDGE, STATS)
TAPS = (((9, C, C), BF16), ((3, C, C), BF16))


def run(kernel, place, args, outs, name, sources=()):
    vmem = pl.BlockSpec(memory_space=pltpu.VMEM)
    hbm = pl.BlockSpec(memory_space=pltpu.HBM)
    return pl.pallas_call(
        kernel,
        out_shape=tuple(jax.ShapeDtypeStruct(s, d) for s, d in outs),
        in_specs=[pl.BlockSpec(memory_space=pltpu.SMEM)]
        + [vmem] * len(args)
        + [hbm] * len(sources),
        out_specs=tuple(vmem for _ in outs),
        scratch_shapes=[pltpu.SemaphoreType.DMA((3,))] if sources else [],
        name=name,
        compiler_params=pltpu.CompilerParams(vmem_limit_bytes=VMEM_LIMIT),
    )(place, *args, *sources)


def weight_grad_kernel(place, *refs):
    lists, (keep_ref, give_ref), scratch = refs[:16], refs[16:18], refs[18:]
    bufs, spatial, temporal, chunks, sems = scratch[:4], *scratch[4:]
    segment, core, half = place[0], place[1], place[2]
    for k in range(4):

        @pl.when(segment == k)
        def _(k=k):
            jobs = [
                pltpu.make_async_copy(lists[4 * k + n], bufs[n], sems.at[n]) for n in range(4)
            ]
            for job in jobs:
                job.start()
            for job in jobs:
                job.wait()

    x, hg, act, u = bufs
    wide = shifted_columns(x[...].astype(F32))
    hidden_grad = hg[...]
    gap = jnp.zeros((PITCH, C), BF16)
    spread_grad = jnp.concatenate([hidden_grad[:PLANE], gap, hidden_grad[PLANE:]], axis=0)
    over_cells = (((0,), (0,)), ((), ()))
    for a in range(3):
        spatial[3 * C * a : 3 * C * (a + 1)] = lax.dot_general(
            wide[a * PITCH : a * PITCH + SPAN], spread_grad, over_cells, preferred_element_type=F32
        )
    upstream = u[...]
    for k in range(3):
        temporal[C * k : C * (k + 1)] = lax.dot_general(
            act[k * PLANE : k * PLANE + CELLS], upstream, over_cells, preferred_element_type=F32
        )
    for n in range(2 * PEERS):
        both = []
        for m in (2 * n, 2 * n + 1):
            both += [spatial[45 * m : 45 * m + 45], temporal[15 * m : 15 * m + 15]]
        both = jnp.concatenate(both, axis=0)
        chunks[n] = both.astype(BF16)
    for q in range(PEERS // 2):
        keep_ref[q] = chunks[4 * q + 2 * core + half]
        give_ref[q, :, :C] = chunks[4 * q + 2 * (1 - core) + half]
        give_ref[q, :, C:] = jnp.zeros((120, PADDED - C), BF16)


def weight_grads(place, kept):
    hbm = pl.BlockSpec(memory_space=pltpu.HBM)
    vmem = pl.BlockSpec(memory_space=pltpu.VMEM)
    lists = [state[name] for state in kept for name in ("x", "hg", "act", "u")]
    chunks = [jax.ShapeDtypeStruct((PEERS // 2, 120, c), BF16) for c in (C, PADDED)]
    return pl.pallas_call(
        weight_grad_kernel,
        out_shape=tuple(chunks),
        in_specs=[pl.BlockSpec(memory_space=pltpu.SMEM)] + [hbm] * 16,
        out_specs=(vmem, vmem),
        scratch_shapes=[
            pltpu.VMEM((CELLS, C), BF16),
            pltpu.VMEM((CELLS, C), BF16),
            pltpu.VMEM(((F_DEV + 2) * PLANE, C), BF16),
            pltpu.VMEM((CELLS, C), BF16),
            pltpu.VMEM((9 * C, C), F32),
            pltpu.VMEM((3 * C, C), F32),
            pltpu.VMEM((2 * PEERS, 120, C), BF16),
            pltpu.SemaphoreType.DMA((4,)),
        ],
        name="weight_grads",
        compiler_params=pltpu.CompilerParams(vmem_limit_bytes=56 * 1024 * 1024),
    )(place, *lists)


def core_sum_kernel(place, keep, got, mine, theirs):
    for q in range(PEERS // 2):
        total = keep[q].astype(F32) + got[q, :, :C].astype(F32)
        low, high = total[:60], total[60:]
        first = place[3] == 0
        mine[q] = jnp.where(first, low, high).astype(BF16)
        theirs[q] = jnp.where(first, high, low).astype(BF16)


def row_sum_kernel(place, mine, got, out):
    for q in range(PEERS // 2):
        out[q] = (mine[q].astype(F32) + got[q].astype(F32)).astype(BF16)


def frame_sum_kernel(place, got, spatial, temporal):
    total = got[0].astype(F32)
    for q in range(1, PEERS // 2):
        total = total + got[q].astype(F32)
    spatial[...] = total[:45]
    temporal[...] = total[45:]


def time_features(timesteps):
    half_dim = TE // 2
    frequency = jnp.exp(-jnp.log(10000.0) * jnp.arange(half_dim).astype(jnp.float32) / half_dim)
    angles = timesteps.astype(jnp.float32)[:, None] * frequency[None, :]
    wave_parts = jnp.concatenate([jnp.cos(angles), jnp.sin(angles)], axis=1)
    return jax.nn.silu(wave_parts).astype(jnp.bfloat16)


def whole_frames(arrays):
    rows = lax.axis_size("row")
    split = jnp.stack([jnp.stack([array[r % CLIPS] for array in arrays]) for r in range(rows)])
    got = lax.all_to_all(split, "row", 0, 0)
    got = jnp.transpose(got, (1, 2, 0, 3, 4, 5)).reshape(len(arrays), F_DEV, ROWS, WIDTH, C)
    got = jnp.pad(got, ((0, 0), (0, 0), (0, 0), (0, PITCH - WIDTH), (0, 0)))
    return [part.reshape(CELLS, C) for part in got]


def exchange(stats):
    return lax.all_to_all(stats, "frame", 0, 0)


def halo(low, high):
    up = [(i, i + 1) for i in range(PEERS - 1)]
    before = lax.ppermute(high, "frame", up)
    after = lax.ppermute(low, "frame", [(j, i) for i, j in up])
    return before, after


def from_segment_zero(array, segment_index, sections):
    got = [lax.ppermute(array, "segment", [(0, j)]) for j in range(1, sections)]
    return jnp.where(segment_index == 0, array, sum(got[1:], got[0]))


def pick(options, segment_index):
    out = options[0]
    for k in range(1, len(options)):
        out = jnp.where(segment_index == k, options[k], out)
    return out


def per_device(
    latents,
    cotangent,
    timesteps,
    frame_counts,
    spatial_weight,
    temporal_weight,
    time_weight,
    norm_gain,
):
    sections = lax.axis_size("segment")
    segment_index = lax.axis_index("segment")
    frame_index = lax.axis_index("frame")
    row_index = lax.axis_index("row")
    clip = row_index % CLIPS
    core = frame_index % 2
    kernel = spatial_weight[0]
    tkernel = temporal_weight[0]

    limit = lax.dynamic_index_in_dim(frame_counts, clip, 0, keepdims=False)
    first = frame_index * F_DEV

    def place_of(k):
        back = (segment_index - k) % sections
        return jnp.stack([first, limit, back, core]).astype(jnp.int32)

    place = place_of(0)

    half = jnp.where(core == 0, kernel[:6], jnp.concatenate([kernel[6:], tkernel], axis=0))
    x, cot = whole_frames((latents, cotangent))
    near = lax.ppermute(half, "segment", [(1, 2), (2, 3), (3, 0)])
    far = lax.ppermute(half, "segment", [(1, 0), (2, 1), (3, 2)])
    swap = [(i, i ^ 1) for i in range(PEERS)]

    time_embed = time_features(timesteps)
    biases = jnp.dot(time_embed, time_weight[0], preferred_element_type=jnp.float32)
    own_rows = jnp.concatenate([biases, norm_gain, jnp.zeros((5, C), F32)], axis=0)
    own_bias = jnp.where(clip == 0, biases[0:1], biases[1:2])

    hidden, low, high, stats = run(conv_kernel, place, (x, kernel, own_bias), CONV_OUT, "conv0")
    before, after = halo(low, high)
    gathered = exchange(stats)
    gathered, near, far = lax.optimization_barrier((gathered, near, far))
    onward = [
        (s * PEERS + f, (s + 1) % sections * PEERS + f) for s in (2, 3, 0) for f in range(0, PEERS, 2)
    ] + [
        (s * PEERS + f, (s - 1) % sections * PEERS + f) for s in (0, 1, 2) for f in range(1, PEERS, 2)
    ]
    on = lax.ppermute(jnp.where(core == 0, near, far), ("segment", "frame"), onward)
    act, moments, out = run(
        output_kernel,
        place,
        (before, hidden, after, gathered, norm_gain, x, tkernel),
        (EXT, ROW8, ACT),
        "output0",
    )
    kept = [dict(x=x, hidden=hidden, act=act, moments=moments)]
    out, near, far, own_rows, cot = lax.optimization_barrier((out, near, far, own_rows, cot))
    x = from_segment_zero(out, segment_index, sections)
    near_other = lax.ppermute(near, "frame", swap)
    far_other = lax.ppermute(far, "frame", swap)
    rows_from = [own_rows]
    for d in range(1, sections):
        pairs = [(k, (k + d) % sections) for k in range(sections)]
        rows_from.append(lax.ppermute(own_rows, "segment", pairs))
    def rows_of(k):
        rows = pick(rows_from, (segment_index - k) % sections)
        bias = jnp.where(clip == 0, rows[0:1], rows[1:2])
        return bias, rows[2:3]

    ids = first + jnp.arange(F_DEV)
    used = jnp.repeat(ids < limit, PLANE)[:, None]
    cot = jnp.where(used, cot, jnp.zeros_like(cot))
    sides = halo(cot[:PLANE], cot[CELLS - PLANE :])
    small = [rows_of(k) + (place_of(k),) for k in range(1, sections)]
    side_place = jnp.stack([segment_index, core, row_index // 2, row_index % 2]).astype(jnp.int32)
    x, on, cot, sides, small, side_place = lax.optimization_barrier(
        (x, on, cot, sides, small, side_place)
    )
    cot_before, cot_after = sides
    on_other = lax.ppermute(on, "frame", swap)
    sources = (kernel, tkernel, near, near_other, far, far_other, on, on_other)

    skip = x
    weights = [(kernel, tkernel)]
    gains = [norm_gain]
    for k in range(1, sections):
        bias, gain, its_place = small[k - 1]
        gains.append(gain)
        if k == 1:
            hidden, low, high, stats, *taps = run(
                fetched_conv_kernel, its_place, (x, bias), CONV_OUT + TAPS, "conv1", sources
            )
        else:
            joins = k == sections - 1
            args = (before, hidden, after, gathered, gains[k - 1], x, weights[k - 1][1], bias)
            args += (skip,) if joins else ()
            act, moments, x, hidden, low, high, stats, *taps = run(
                functools.partial(section_kernel, joins),
                its_place,
                args,
                (EXT, ROW8, ACT) + CONV_OUT + TAPS,
                f"section{k}",
                sources,
            )
            kept[k - 1].update(act=act, moments=moments)
        weights.append(taps)
        kept.append(dict(x=x, hidden=hidden))
        before, after = halo(low, high)
        gathered = exchange(stats)

    u, u_before, u_after = cot, cot_before, cot_after
    skip_u = None
    for k in reversed(range(sections)):
        state = kept[k]
        sides = (u_before, u, u_after)
        if k == sections - 1:
            act, moments, grad, sums = run(
                functools.partial(act_grad_kernel, "last"),
                place,
                sides + (before, state["hidden"], after, gathered, gains[k], weights[k][1]),
                (EXT, ROW8, HID, STATS),
                "act_grad_last",
            )
            state.update(act=act, moments=moments)
        elif k == 0:
            u, grad, sums = run(
                functools.partial(act_grad_kernel, "first"),
                place,
                sides + skip_u + (state["hidden"], state["moments"], gains[k], weights[k][1]),
                (ACT, HID, STATS),
                "act_grad_first",
            )
        else:
            grad, sums = run(
                functools.partial(act_grad_kernel, "mid"),
                place,
                sides + (state["hidden"], state["moments"], gains[k], weights[k][1]),
                (HID, STATS),
                f"act_grad{k}",
            )
        state.update(u=u)
        sums = exchange(sums)
        args = (grad, state["hidden"], state["moments"], sums)
        if k > 0:
            hg, col, u, low, high = run(
                input_grad_kernel,
                place,
                args + (u, weights[k][0]),
                (ACT, ROW8, ACT, EDGE, EDGE),
                f"input_grad{k}",
            )
            u_before, u_after = halo(low, high)
            if k == sections - 1:
                skip_u = (u_before, u, u_after)
        else:
            hg, col = run(hidden_grad_kernel, place, args, (ACT, ROW8), "hidden_grad0")
        state.update(hg=hg, col=col)

    partner = [(i, i ^ 1) for i in range(4)]
    keep, give = weight_grads(side_place, kept)
    got = lax.ppermute(give, "frame", swap)
    col = pick([state["col"] for state in kept], segment_index)
    other = lax.ppermute(col, "row", partner)
    chunk = ((PEERS // 2, 60, C), BF16)
    keep, give = run(core_sum_kernel, side_place, (keep, got), (chunk, chunk), "core_sum")
    got = lax.ppermute(give, "row", partner)
    (summed,) = run(row_sum_kernel, side_place, (keep, got), (chunk,), "row_sum")
    groups = [[i for i in range(PEERS) if i % 2 == c] for c in range(2)]
    got = lax.all_to_all(summed, "frame", 0, 0, axis_index_groups=groups)
    spatial_out, temporal_out = run(
        frame_sum_kernel, side_place, (got,), (((45, C), F32), ((15, C), F32)), "frame_sum"
    )

    peers = 4 * PEERS
    gain_total = col[1] + other[1]
    totals = [jnp.where(clip == c, col[0], other[0]) for c in range(CLIPS)]
    spot = frame_index * 4 + row_index
    gain_out = lax.dynamic_slice_in_dim(gain_total, spot * (C // peers), C // peers)
    features = lax.dynamic_slice_in_dim(time_embed, spot * (TE // peers), TE // peers, axis=1)
    features = features.astype(F32)
    time_out = sum(features[c][:, None] * totals[c][None, :] for c in range(CLIPS))
    return (spatial_out[None], temporal_out[None], time_out[None], gain_out[None])


def solution(mesh):
    return jax.shard_map(
        per_device,
        mesh=mesh,
        in_specs=(
            P(None, "frame", "row", None, None),
            P(None, "frame", "row", None, None),
            P(),
            P(),
            P("segment", None, None, None),
            P("segment", None, None, None),
            P("segment", None, None),
            P("segment", None),
        ),
        out_specs=(
            P("segment", ("frame", "row"), None),
            P("segment", ("frame", "row"), None),
            P("segment", ("frame", "row"), None),
            P("segment", ("frame", "row")),
        ),
        check_vma=False,
    )
```

```python
import functools

import jax
import jax.numpy as jnp
from jax import lax
from jax.experimental import pallas as pl
from jax.experimental.pallas import tpu as pltpu
from jax.sharding import PartitionSpec as P


C = 320
G = 32
TE = 1280
WIDTH = 24
PITCH = 32
ROWS = 8
F_DEV = 2
CLIPS = 2
EPSILON = 1e-05

PLANE = ROWS * PITCH
CELLS = F_DEV * PLANE
UNIT = float(ROWS * WIDTH * (C // G))
PEERS = 16
PADDED = 384
VMEM_LIMIT = 20 * 1024 * 1024
F32 = jnp.float32
BF16 = jnp.bfloat16


def dot(a, b):
    return jnp.dot(a, b, preferred_element_type=F32)


def dot_back(a, b):
    return lax.dot_general(a, b, (((1,), (1,)), ((), ())), preferred_element_type=F32)


def exact_dot(a, b):
    return jnp.dot(a, b, preferred_element_type=F32, precision=lax.Precision.HIGHEST)


def to_groups():
    ch = lax.broadcasted_iota(jnp.int32, (C, 128), 0)
    low = lax.broadcasted_iota(jnp.int32, (C, 128), 1) * (C // G)
    return ((ch >= low) & (ch < low + C // G)).astype(F32)


def to_channels():
    ch = lax.broadcasted_iota(jnp.int32, (128, C), 1)
    low = lax.broadcasted_iota(jnp.int32, (128, C), 0) * (C // G)
    return ((ch >= low) & (ch < low + C // G)).astype(F32)


def col_mask(rows):
    at = lax.broadcasted_iota(jnp.int32, (rows, 1), 0)
    return (jnp.bitwise_and(at, PITCH - 1) < WIDTH).astype(F32)


def live_mask(first, limit, frames):
    parts = []
    for f in range(frames):
        ok = jnp.where((first + f >= 0) & (first + f < limit), 1.0, 0.0)
        parts.append(jnp.full((PLANE, 1), 1.0, F32) * ok)
    return jnp.concatenate(parts, axis=0) * col_mask(frames * PLANE)


def two_rows(top, second):
    return jnp.concatenate([top, second, jnp.zeros((6, top.shape[1]), F32)], axis=0)


def shifted_columns(x):
    rows = x.shape[0]
    gap = jnp.zeros((PITCH, 3 * C), BF16)
    wide = jnp.concatenate(
        [
            pltpu.roll(x, 1, 0).astype(BF16),
            x.astype(BF16),
            pltpu.roll(x, rows - 1, 0).astype(BF16),
        ],
        axis=1,
    )
    return jnp.concatenate([gap, wide[:PLANE], gap, wide[PLANE:], gap], axis=0)


SPAN = CELLS + PITCH


def without_gap(x):
    return jnp.concatenate([x[:PLANE], x[PLANE + PITCH :]], axis=0)


def conv(x, w_ref):
    wide = shifted_columns(x)
    total = None
    for a in range(3):
        taps = w_ref[3 * a : 3 * a + 3].reshape(3 * C, C)
        part = dot(wide[a * PITCH : a * PITCH + SPAN], taps)
        total = part if total is None else total + part
    return without_gap(total)


def conv_back(x, w_ref):
    wide = shifted_columns(x)
    total = None
    for a in range(3):
        taps = jnp.concatenate([w_ref[3 * a + 2], w_ref[3 * a + 1], w_ref[3 * a]], axis=1)
        part = dot_back(wide[(2 - a) * PITCH : (2 - a) * PITCH + SPAN], taps)
        total = part if total is None else total + part
    return without_gap(total)


def joined_stats(gathered_ref, limit):
    means = gathered_ref[:, 0, :]
    squares = gathered_ref[:, 1, :]
    peer = lax.broadcasted_iota(jnp.int32, (PEERS, 128), 0)
    held = jnp.clip(limit - peer * F_DEV, 0, F_DEV).astype(F32) * UNIT
    total = limit.astype(F32) * UNIT
    mean = jnp.sum(held * means, axis=0, keepdims=True) / total
    apart = means - mean
    variance = jnp.sum(squares + held * apart * apart, axis=0, keepdims=True) / total
    both = exact_dot(two_rows(mean, lax.rsqrt(variance + EPSILON)), to_channels())
    sums = from_lanes(jnp.sum(gathered_ref[...], axis=0), 2) * both[1:2]
    return jnp.concatenate([both[0:2], sums, jnp.zeros((5, C), F32)], axis=0)


def in_lanes(row):
    tail = jnp.concatenate([row[:, 256:], jnp.zeros((1, 3 * 128 - C), F32)], axis=1)
    return [row[:, :128], row[:, 128:256], tail]


def from_lanes(sums, at):
    parts = [sums[at : at + 1], sums[at + 1 : at + 2], sums[at + 2 : at + 3, : C - 256]]
    return jnp.concatenate(parts, axis=1)


def own_stats(hidden, mask, first, limit):
    held = jnp.clip(limit - first, 0, F_DEV).astype(F32) * UNIT
    sums = jnp.sum(hidden * mask, axis=0, keepdims=True)
    pad = jnp.zeros_like(sums)
    mean = exact_dot(two_rows(sums, pad), to_groups()) / jnp.maximum(held, 1.0)
    off = hidden - exact_dot(mean, to_channels())[0:1]
    square = jnp.sum(off * off * mask, axis=0, keepdims=True)
    square = exact_dot(two_rows(pad, square), to_groups())
    by_channel = jnp.sum(off * mask, axis=0, keepdims=True)
    rest = [jnp.zeros((3, 128), F32)]
    return jnp.concatenate([mean[0:1], square[1:2]] + in_lanes(by_channel) + rest, axis=0)


def put_stats(stats, out_ref):
    for peer in range(PEERS):
        out_ref[peer] = stats


def put_edges(value, low_ref, high_ref):
    low_ref[...] = value[:PLANE]
    high_ref[...] = value[CELLS - PLANE :]


def conv_kernel(place, x_ref, w_ref, bias_ref, hidden_ref, low_ref, high_ref, stats_ref):
    hidden = conv(x_ref[...].astype(F32), w_ref) + bias_ref[...]
    hidden_ref[...] = hidden
    put_edges(hidden, low_ref, high_ref)
    first, limit = place[0], place[1]
    put_stats(own_stats(hidden, live_mask(first, limit, F_DEV), first, limit), stats_ref)


def activate(place, hidden, moments, gain, frames_before, frames):
    normed = (hidden - moments[0:1]) * moments[1:2]
    scaled = normed * gain
    mask = live_mask(place[0] - frames_before, place[1], frames)
    return (mask * (scaled * jax.nn.sigmoid(scaled))).astype(BF16)


def activate_all(place, before_ref, hidden_ref, after_ref, gathered_ref, gain_ref, act_ref, moments_ref):
    moments = joined_stats(gathered_ref, place[1])
    moments_ref[...] = moments
    gain = gain_ref[...]
    act_ref[:PLANE] = activate(place, before_ref[...], moments, gain, 1, 1)
    act_ref[PLANE : PLANE + CELLS] = activate(place, hidden_ref[...], moments, gain, 0, F_DEV)
    act_ref[PLANE + CELLS :] = activate(place, after_ref[...], moments, gain, -F_DEV, 1)


def section_output(act_ref, x_ref, t_ref):
    wide = jnp.concatenate([act_ref[k * PLANE : k * PLANE + CELLS] for k in range(3)], axis=1)
    temporal = dot(wide, t_ref[...].reshape(3 * C, C))
    return (x_ref[...].astype(F32) + temporal).astype(BF16)


def output_kernel(
    place, before, hidden, after, gathered, gain, x, t, act_ref, moments_ref, out_ref
):
    activate_all(place, before, hidden, after, gathered, gain, act_ref, moments_ref)
    out_ref[...] = section_output(act_ref, x, t)


def fetch(place, sources, w_out, t_out, sems, begin):
    w, t, near, near_other, far, far_other, on, on_other = sources
    back, core = place[2], place[3]

    def go(*pairs):
        for n, (source, target) in enumerate(pairs):
            job = pltpu.make_async_copy(source, target, sems.at[n])
            if begin:
                job.start()
            else:
                job.wait()

    @pl.when(back == 0)
    def _():
        go((w, w_out), (t, t_out))

    for d, held in ((1, (near, near_other)), (2, (on, on_other)), (3, (far, far_other))):
        for c in range(2):

            @pl.when((back == d) & (core == c))
            def _(lower=held[c], upper=held[1 - c]):
                go(
                    (lower, w_out.at[pl.ds(0, 6)]),
                    (upper.at[pl.ds(0, 3)], w_out.at[pl.ds(6, 3)]),
                    (upper.at[pl.ds(3, 3)], t_out),
                )


def fetched_conv_kernel(place, x, bias, *rest):
    sources, (hidden_ref, low, high, stats, w_out, t_out) = rest[:8], rest[8:14]
    sems = rest[14]
    fetch(place, sources, w_out, t_out, sems, True)
    fetch(place, sources, w_out, t_out, sems, False)
    conv_kernel(place, x, w_out, bias, hidden_ref, low, high, stats)


def section_kernel(joins, place, before, hidden, after, gathered, gain, x, t, bias, *rest):
    if joins:
        skip, rest = rest[0], rest[1:]
    sources, rest = rest[:8], rest[8:]
    act_ref, moments_ref, out_ref, hidden_ref, low, high, stats_ref, w_out, t_out = rest[:9]
    sems = rest[9]
    fetch(place, sources, w_out, t_out, sems, True)
    activate_all(place, before, hidden, after, gathered, gain, act_ref, moments_ref)
    out = section_output(act_ref, x, t)
    if joins:
        out = (out.astype(F32) + skip[...].astype(F32)).astype(BF16)
    out_ref[...] = out
    fetch(place, sources, w_out, t_out, sems, False)
    conv_kernel(place, out_ref, w_out, bias, hidden_ref, low, high, stats_ref)


def act_grad_kernel(
    mode, place, u_before, u, u_after, *rest
):
    first, limit = place[0], place[1]
    if mode == "last":
        (before, hidden, after, gathered, gain_ref, t, act_ref, moments_ref, grad_ref, sums_ref) = rest
        activate_all(place, before, hidden, after, gathered, gain_ref, act_ref, moments_ref)
        planes = [u_before[...], u[...], u_after[...]]
    elif mode == "first":
        (s_before, s, s_after, hidden, moments_ref, gain_ref, t, u_out, grad_ref, sums_ref) = rest
        planes = [
            (p[...].astype(F32) + q[...].astype(F32)).astype(BF16)
            for p, q in ((u_before, s_before), (u, s), (u_after, s_after))
        ]
        u_out[...] = planes[1]
    else:
        hidden, moments_ref, gain_ref, t, grad_ref, sums_ref = rest
        planes = [u_before[...], u[...], u_after[...]]
    ext = jnp.concatenate(planes, axis=0)
    wide = jnp.concatenate([ext[(2 - k) * PLANE : (2 - k) * PLANE + CELLS] for k in range(3)], axis=1)
    taps = jnp.concatenate([t[0], t[1], t[2]], axis=1)
    act_grad = dot_back(wide, taps)
    gain = gain_ref[...]
    normed = (hidden[...] - moments_ref[0:1]) * moments_ref[1:2]
    scaled = normed * gain
    gate = jax.nn.sigmoid(scaled)
    scaled_grad = act_grad * live_mask(first, limit, F_DEV) * gate * (1.0 + scaled * (1.0 - gate))
    by_normed = jnp.sum(scaled_grad * normed, axis=0, keepdims=True)
    grad = scaled_grad * gain
    grad_ref[...] = grad
    plain = jnp.sum(grad, axis=0, keepdims=True)
    groups = exact_dot(two_rows(plain, by_normed * gain), to_groups())
    rows = [groups[0:2]] + in_lanes(plain) + in_lanes(by_normed)
    put_stats(jnp.concatenate(rows, axis=0), sums_ref)


def hidden_grad(place, grad_ref, hidden_ref, moments_ref, sums_ref, hg_ref, col_ref):
    first, limit = place[0], place[1]
    total = limit.astype(F32) * UNIT
    sums = jnp.sum(sums_ref[...], axis=0)
    means = exact_dot(sums, to_channels()) / total
    normed = (hidden_ref[...] - moments_ref[0:1]) * moments_ref[1:2]
    mask = live_mask(first, limit, F_DEV)
    hg = moments_ref[1:2] * (grad_ref[...] - mask * (means[0:1] + normed * means[1:2]))
    hg = hg.astype(BF16)
    hg_ref[...] = hg
    cells = limit.astype(F32) * (ROWS * WIDTH)
    col = from_lanes(sums, 2) - means[0:1] * cells - means[1:2] * moments_ref[2:3]
    col_ref[...] = two_rows(moments_ref[1:2] * col, from_lanes(sums, 5))
    return hg.astype(F32)


def input_grad_kernel(place, grad, hidden, moments, sums, u, w, hg_ref, col_ref, out_ref, low, high):
    hg = hidden_grad(place, grad, hidden, moments, sums, hg_ref, col_ref)
    out = u[...].astype(F32) + conv_back(hg, w)
    out = (out * col_mask(CELLS)).astype(BF16)
    out_ref[...] = out
    put_edges(out, low, high)


def hidden_grad_kernel(place, grad, hidden, moments, sums, hg_ref, col_ref):
    hidden_grad(place, grad, hidden, moments, sums, hg_ref, col_ref)


ACT = ((CELLS, C), BF16)
HID = ((CELLS, C), F32)
EXT = (((F_DEV + 2) * PLANE, C), BF16)
ROW8 = ((8, C), F32)
STATS = ((PEERS, 8, 128), F32)


EDGE = ((PLANE, C), BF16)
WIDE_EDGE = ((PLANE, C), F32)
CONV_OUT = (HID, WIDE_EDGE, WIDE_EDGE, STATS)
TAPS = (((9, C, C), BF16), ((3, C, C), BF16))


def run(kernel, place, args, outs, sources=()):
    vmem = pl.BlockSpec(memory_space=pltpu.VMEM)
    hbm = pl.BlockSpec(memory_space=pltpu.HBM)
    return pl.pallas_call(
        kernel,
        out_shape=tuple(jax.ShapeDtypeStruct(s, d) for s, d in outs),
        in_specs=[pl.BlockSpec(memory_space=pltpu.SMEM)]
        + [vmem] * len(args)
        + [hbm] * len(sources),
        out_specs=tuple(vmem for _ in outs),
        scratch_shapes=[pltpu.SemaphoreType.DMA((3,))] if sources else [],
        compiler_params=pltpu.CompilerParams(vmem_limit_bytes=VMEM_LIMIT),
    )(place, *args, *sources)


def weight_grad_kernel(place, *refs):
    lists, (keep_ref, give_ref), scratch = refs[:16], refs[16:18], refs[18:]
    bufs, wide_ref, spatial, temporal, chunks, sems = scratch[:4], *scratch[4:]
    segment, core, half = place[0], place[1], place[2]
    for k in range(4):

        @pl.when(segment == k)
        def _(k=k):
            jobs = [
                pltpu.make_async_copy(lists[4 * k + n], bufs[n], sems.at[n]) for n in range(4)
            ]
            for job in jobs:
                job.start()
            for job in jobs:
                job.wait()

    x, hg, act, u = bufs
    wide_ref[...] = shifted_columns(x[...].astype(F32))
    hidden_grad = hg[...]
    gap = jnp.zeros((PITCH, C), BF16)
    spread_grad = jnp.concatenate([hidden_grad[:PLANE], gap, hidden_grad[PLANE:]], axis=0)
    upstream = u[...]
    over_cells = (((0,), (0,)), ((), ()))

    def taps(k, carry):
        rows = wide_ref[pl.ds(pl.multiple_of(k * PITCH, PITCH), SPAN), :]
        spatial[pl.ds(pl.multiple_of(3 * C * k, 8), 3 * C)] = lax.dot_general(
            rows, spread_grad, over_cells, preferred_element_type=F32
        )
        rows = act[pl.ds(pl.multiple_of(k * PLANE, PLANE), CELLS), :]
        temporal[pl.ds(pl.multiple_of(C * k, 8), C)] = lax.dot_general(
            rows, upstream, over_cells, preferred_element_type=F32
        )
        return carry

    lax.fori_loop(0, 3, taps, 0)

    def cut(n, carry):
        rows = spatial[pl.ds(pl.multiple_of(720 * n, 8), 720), :]
        more = temporal[pl.ds(pl.multiple_of(240 * n, 8), 240), :]
        for m in range(8):
            both = []
            for p in (2 * m, 2 * m + 1):
                both += [rows[45 * p : 45 * p + 45], more[15 * p : 15 * p + 15]]
            chunks[8 * n + m] = jnp.concatenate(both, axis=0).astype(BF16)
        return carry

    lax.fori_loop(0, 4, cut, 0)
    for q in range(PEERS // 2):
        keep_ref[q] = chunks[4 * q + 2 * core + half]
        give_ref[q, :, :C] = chunks[4 * q + 2 * (1 - core) + half]
        give_ref[q, :, C:] = jnp.zeros((120, PADDED - C), BF16)


def weight_grads(place, kept):
    hbm = pl.BlockSpec(memory_space=pltpu.HBM)
    vmem = pl.BlockSpec(memory_space=pltpu.VMEM)
    lists = [state[name] for state in kept for name in ("x", "hg", "act", "u")]
    chunks = [jax.ShapeDtypeStruct((PEERS // 2, 120, c), BF16) for c in (C, PADDED)]
    return pl.pallas_call(
        weight_grad_kernel,
        out_shape=tuple(chunks),
        in_specs=[pl.BlockSpec(memory_space=pltpu.SMEM)] + [hbm] * 16,
        out_specs=(vmem, vmem),
        scratch_shapes=[
            pltpu.VMEM((CELLS, C), BF16),
            pltpu.VMEM((CELLS, C), BF16),
            pltpu.VMEM(((F_DEV + 2) * PLANE, C), BF16),
            pltpu.VMEM((CELLS, C), BF16),
            pltpu.VMEM((SPAN + 2 * PITCH, 3 * C), BF16),
            pltpu.VMEM((9 * C, C), F32),
            pltpu.VMEM((3 * C, C), F32),
            pltpu.VMEM((2 * PEERS, 120, C), BF16),
            pltpu.SemaphoreType.DMA((4,)),
        ],
        name="weight_grads",
        compiler_params=pltpu.CompilerParams(vmem_limit_bytes=56 * 1024 * 1024),
    )(place, *lists)


def core_sum_kernel(place, keep, got, mine, theirs):
    for q in range(PEERS // 2):
        total = keep[q].astype(F32) + got[q, :, :C].astype(F32)
        low, high = total[:60], total[60:]
        first = place[3] == 0
        mine[q] = jnp.where(first, low, high).astype(BF16)
        theirs[q] = jnp.where(first, high, low).astype(BF16)


def row_sum_kernel(place, mine, got, out):
    for q in range(PEERS // 2):
        out[q] = (mine[q].astype(F32) + got[q].astype(F32)).astype(BF16)


def frame_sum_kernel(place, got, spatial, temporal):
    total = got[0].astype(F32)
    for q in range(1, PEERS // 2):
        total = total + got[q].astype(F32)
    spatial[...] = total[:45]
    temporal[...] = total[45:]


def time_features(timesteps):
    half_dim = TE // 2
    frequency = jnp.exp(-jnp.log(10000.0) * jnp.arange(half_dim).astype(jnp.float32) / half_dim)
    angles = timesteps.astype(jnp.float32)[:, None] * frequency[None, :]
    wave_parts = jnp.concatenate([jnp.cos(angles), jnp.sin(angles)], axis=1)
    return jax.nn.silu(wave_parts).astype(jnp.bfloat16)


def whole_frames(arrays):
    rows = lax.axis_size("row")
    split = jnp.stack([jnp.stack([array[r % CLIPS] for array in arrays]) for r in range(rows)])
    got = lax.all_to_all(split, "row", 0, 0)
    got = jnp.transpose(got, (1, 2, 0, 3, 4, 5)).reshape(len(arrays), F_DEV, ROWS, WIDTH, C)
    got = jnp.pad(got, ((0, 0), (0, 0), (0, 0), (0, PITCH - WIDTH), (0, 0)))
    return [part.reshape(CELLS, C) for part in got]


def exchange(stats):
    return lax.all_to_all(stats, "frame", 0, 0)


def halo(low, high):
    up = [(i, i + 1) for i in range(PEERS - 1)]
    before = lax.ppermute(high, "frame", up)
    after = lax.ppermute(low, "frame", [(j, i) for i, j in up])
    return before, after


def from_segment_zero(array, segment_index, sections):
    got = [lax.ppermute(array, "segment", [(0, j)]) for j in range(1, sections)]
    return jnp.where(segment_index == 0, array, sum(got[1:], got[0]))


def pick(options, segment_index):
    out = options[0]
    for k in range(1, len(options)):
        out = jnp.where(segment_index == k, options[k], out)
    return out


def per_device(
    latents,
    cotangent,
    timesteps,
    frame_counts,
    spatial_weight,
    temporal_weight,
    time_weight,
    norm_gain,
):
    sections = lax.axis_size("segment")
    segment_index = lax.axis_index("segment")
    frame_index = lax.axis_index("frame")
    row_index = lax.axis_index("row")
    clip = row_index % CLIPS
    core = frame_index % 2
    kernel = spatial_weight[0]
    tkernel = temporal_weight[0]

    limit = lax.dynamic_index_in_dim(frame_counts, clip, 0, keepdims=False)
    first = frame_index * F_DEV

    def place_of(k):
        back = (segment_index - k) % sections
        return jnp.stack([first, limit, back, core]).astype(jnp.int32)


    half = jnp.where(core == 0, kernel[:6], jnp.concatenate([kernel[6:], tkernel], axis=0))
    x, cot = whole_frames((latents, cotangent))
    near = lax.ppermute(half, "segment", [(1, 2), (2, 3), (3, 0)])
    far = lax.ppermute(half, "segment", [(1, 0), (2, 1), (3, 2)])
    swap = [(i, i ^ 1) for i in range(PEERS)]

    time_embed = time_features(timesteps)
    biases = jnp.dot(time_embed, time_weight[0], preferred_element_type=jnp.float32)
    own_rows = jnp.concatenate([biases, norm_gain, jnp.zeros((5, C), F32)], axis=0)
    own_bias = jnp.where(clip == 0, biases[0:1], biases[1:2])


    used = jnp.repeat(first + jnp.arange(F_DEV) < limit, PLANE)
    places = [place_of(k) for k in range(sections)]
    side_place = jnp.stack([segment_index, core, row_index // 2, row_index % 2]).astype(jnp.int32)
    x, own_bias, own_rows, used, places, side_place = lax.optimization_barrier(
        (x, own_bias, own_rows, used, places, side_place)
    )
    place = places[0]

    hidden, low, high, stats = run(conv_kernel, place, (x, kernel, own_bias), CONV_OUT)
    before, after = halo(low, high)
    gathered = exchange(stats)
    gathered, near, far = lax.optimization_barrier((gathered, near, far))

    def onward(up, down):
        return [(s * PEERS + f, t * PEERS + f) for s, t in up for f in range(0, PEERS, 2)] + [
            (s * PEERS + f, t * PEERS + f) for s, t in down for f in range(1, PEERS, 2)
        ]

    passed = jnp.where(core == 0, near, far)
    gathered, passed = lax.optimization_barrier((gathered, passed))
    everyone = ("segment", "frame")
    on = lax.ppermute(passed, everyone, onward([(2, 3), (3, 0)], [(0, 3), (1, 0)]))
    act, moments, out = run(
        output_kernel,
        place,
        (before, hidden, after, gathered, norm_gain, x, tkernel),
        (EXT, ROW8, ACT),
    )
    kept = [dict(x=x, hidden=hidden, act=act, moments=moments)]
    out, near, far, cot, own_rows = lax.optimization_barrier((out, near, far, cot, own_rows))
    rows_from = [own_rows]
    x = from_segment_zero(out, segment_index, sections)
    for d in range(1, sections):
        pairs = [(k, (k + d) % sections) for k in range(sections)]
        rows_from.append(lax.ppermute(own_rows, "segment", pairs))
    near_other = lax.ppermute(near, "frame", swap)
    far_other = lax.ppermute(far, "frame", swap)

    def rows_of(k):
        rows = pick(rows_from, (segment_index - k) % sections)
        bias = jnp.where(clip == 0, rows[0:1], rows[1:2])
        return bias, rows[2:3]

    cot = jnp.where(used[:, None], cot, jnp.zeros_like(cot))
    sides = halo(cot[:PLANE], cot[CELLS - PLANE :])
    small = [rows_of(k) + (places[k],) for k in range(1, sections)]
    x, on, cot, sides, small, passed = lax.optimization_barrier((x, on, cot, sides, small, passed))
    cot_before, cot_after = sides
    on_other = lax.ppermute(on, "frame", swap)
    last = lax.ppermute(passed, everyone, onward([(0, 1)], [(2, 1)]))
    fetched = (kernel, tkernel, near, near_other, far, far_other)
    sources = fetched + (on, on_other)

    skip = x
    weights = [(kernel, tkernel)]
    gains = [norm_gain]
    for k in range(1, sections):
        bias, gain, its_place = small[k - 1]
        gains.append(gain)
        if k == 1:
            hidden, low, high, stats, *taps = run(
                fetched_conv_kernel, its_place, (x, bias), CONV_OUT + TAPS, sources
            )
        else:
            joins = k == sections - 1
            args = (before, hidden, after, gathered, gains[k - 1], x, weights[k - 1][1], bias)
            args += (skip,) if joins else ()
            act, moments, x, hidden, low, high, stats, *taps = run(
                functools.partial(section_kernel, joins),
                its_place,
                args,
                (EXT, ROW8, ACT) + CONV_OUT + TAPS,
                sources,
            )
            kept[k - 1].update(act=act, moments=moments)
        weights.append(taps)
        kept.append(dict(x=x, hidden=hidden))
        if k == 2:
            low, last = lax.optimization_barrier((low, last))
        before, after = halo(low, high)
        gathered = exchange(stats)
        if k == 2:
            last_other = lax.ppermute(last, "frame", swap)
            sources = fetched + (last, last_other)

    u, u_before, u_after = cot, cot_before, cot_after
    skip_u = None
    for k in reversed(range(sections)):
        state = kept[k]
        sides = (u_before, u, u_after)
        if k == sections - 1:
            act, moments, grad, sums = run(
                functools.partial(act_grad_kernel, "last"),
                place,
                sides + (before, state["hidden"], after, gathered, gains[k], weights[k][1]),
                (EXT, ROW8, HID, STATS),
            )
            state.update(act=act, moments=moments)
        elif k == 0:
            u, grad, sums = run(
                functools.partial(act_grad_kernel, "first"),
                place,
                sides + skip_u + (state["hidden"], state["moments"], gains[k], weights[k][1]),
                (ACT, HID, STATS),
            )
        else:
            grad, sums = run(
                functools.partial(act_grad_kernel, "mid"),
                place,
                sides + (state["hidden"], state["moments"], gains[k], weights[k][1]),
                (HID, STATS),
            )
        state.update(u=u)
        sums = exchange(sums)
        args = (grad, state["hidden"], state["moments"], sums)
        if k > 0:
            hg, col, u, low, high = run(
                input_grad_kernel, place, args + (u, weights[k][0]), (ACT, ROW8, ACT, EDGE, EDGE)
            )
            u_before, u_after = halo(low, high)
            if k == sections - 1:
                skip_u = (u_before, u, u_after)
        else:
            hg, col = run(hidden_grad_kernel, place, args, (ACT, ROW8))
        state.update(hg=hg, col=col)

    partner = [(i, i ^ 1) for i in range(4)]
    keep, give = weight_grads(side_place, kept)
    got = lax.ppermute(give, "frame", swap)
    col = pick([state["col"] for state in kept], segment_index)
    other = lax.ppermute(col, "row", partner)
    chunk = ((PEERS // 2, 60, C), BF16)
    keep, give = run(core_sum_kernel, side_place, (keep, got), (chunk, chunk))
    got = lax.ppermute(give, "row", partner)
    (summed,) = run(row_sum_kernel, side_place, (keep, got), (chunk,))
    groups = [[i for i in range(PEERS) if i % 2 == c] for c in range(2)]
    got = lax.all_to_all(summed, "frame", 0, 0, axis_index_groups=groups)
    spatial_out, temporal_out = run(
        frame_sum_kernel, side_place, (got,), (((45, C), F32), ((15, C), F32))
    )

    peers = 4 * PEERS
    gain_total = col[1] + other[1]
    totals = [jnp.where(clip == c, col[0], other[0]) for c in range(CLIPS)]
    spot = frame_index * 4 + row_index
    gain_out = lax.dynamic_slice_in_dim(gain_total, spot * (C // peers), C // peers)
    features = lax.dynamic_slice_in_dim(time_embed, spot * (TE // peers), TE // peers, axis=1)
    features = features.astype(F32)
    time_out = sum(features[c][:, None] * totals[c][None, :] for c in range(CLIPS))
    return (spatial_out[None], temporal_out[None], time_out[None], gain_out[None])


def solution(mesh):
    return jax.shard_map(
        per_device,
        mesh=mesh,
        in_specs=(
            P(None, "frame", "row", None, None),
            P(None, "frame", "row", None, None),
            P(),
            P(),
            P("segment", None, None, None),
            P("segment", None, None, None),
            P("segment", None, None),
            P("segment", None),
        ),
        out_specs=(
            P("segment", ("frame", "row"), None),
            P("segment", ("frame", "row"), None),
            P("segment", ("frame", "row"), None),
            P("segment", ("frame", "row")),
        ),
        check_vma=False,
    )
```

```python
import functools

import jax
import jax.numpy as jnp
from jax import lax
from jax.experimental import pallas as pl
from jax.experimental.pallas import tpu as pltpu
from jax.sharding import PartitionSpec as P


C = 320
G = 32
TE = 1280
WIDTH = 24
PITCH = 32
ROWS = 8
F_DEV = 2
CLIPS = 2
EPSILON = 1e-05

PLANE = ROWS * PITCH
CELLS = F_DEV * PLANE
UNIT = float(ROWS * WIDTH * (C // G))
PEERS = 16
PADDED = 384
VMEM_LIMIT = 20 * 1024 * 1024
F32 = jnp.float32
BF16 = jnp.bfloat16


def dot(a, b):
    return jnp.dot(a, b, preferred_element_type=F32)


def dot_back(a, b):
    return lax.dot_general(a, b, (((1,), (1,)), ((), ())), preferred_element_type=F32)


def exact_dot(a, b):
    return jnp.dot(a, b, preferred_element_type=F32, precision=lax.Precision.HIGHEST)


def to_groups():
    ch = lax.broadcasted_iota(jnp.int32, (C, 128), 0)
    low = lax.broadcasted_iota(jnp.int32, (C, 128), 1) * (C // G)
    return ((ch >= low) & (ch < low + C // G)).astype(F32)


def to_channels():
    ch = lax.broadcasted_iota(jnp.int32, (128, C), 1)
    low = lax.broadcasted_iota(jnp.int32, (128, C), 0) * (C // G)
    return ((ch >= low) & (ch < low + C // G)).astype(F32)


def col_mask(rows):
    at = lax.broadcasted_iota(jnp.int32, (rows, 1), 0)
    return (jnp.bitwise_and(at, PITCH - 1) < WIDTH).astype(F32)


def live_mask(first, limit, frames):
    parts = []
    for f in range(frames):
        ok = jnp.where((first + f >= 0) & (first + f < limit), 1.0, 0.0)
        parts.append(jnp.full((PLANE, 1), 1.0, F32) * ok)
    return jnp.concatenate(parts, axis=0) * col_mask(frames * PLANE)


def two_rows(top, second):
    return jnp.concatenate([top, second, jnp.zeros((6, top.shape[1]), F32)], axis=0)


def shifted_columns(x):
    rows = x.shape[0]
    gap = jnp.zeros((PITCH, 3 * C), BF16)
    wide = jnp.concatenate(
        [
            pltpu.roll(x, 1, 0).astype(BF16),
            x.astype(BF16),
            pltpu.roll(x, rows - 1, 0).astype(BF16),
        ],
        axis=1,
    )
    return jnp.concatenate([gap, wide[:PLANE], gap, wide[PLANE:], gap], axis=0)


SPAN = CELLS + PITCH


def without_gap(x):
    return jnp.concatenate([x[:PLANE], x[PLANE + PITCH :]], axis=0)


def conv(x, w_ref):
    wide = shifted_columns(x)
    total = None
    for a in range(3):
        taps = w_ref[3 * a : 3 * a + 3].reshape(3 * C, C)
        part = dot(wide[a * PITCH : a * PITCH + SPAN], taps)
        total = part if total is None else total + part
    return without_gap(total)


def conv_back(x, w_ref):
    wide = shifted_columns(x)
    total = None
    for a in range(3):
        taps = jnp.concatenate([w_ref[3 * a + 2], w_ref[3 * a + 1], w_ref[3 * a]], axis=1)
        part = dot_back(wide[(2 - a) * PITCH : (2 - a) * PITCH + SPAN], taps)
        total = part if total is None else total + part
    return without_gap(total)


def joined_stats(gathered_ref, limit):
    means = gathered_ref[:, 0, :]
    squares = gathered_ref[:, 1, :]
    peer = lax.broadcasted_iota(jnp.int32, (PEERS, 128), 0)
    held = jnp.clip(limit - peer * F_DEV, 0, F_DEV).astype(F32) * UNIT
    total = limit.astype(F32) * UNIT
    mean = jnp.sum(held * means, axis=0, keepdims=True) / total
    apart = means - mean
    variance = jnp.sum(squares + held * apart * apart, axis=0, keepdims=True) / total
    both = exact_dot(two_rows(mean, lax.rsqrt(variance + EPSILON)), to_channels())
    sums = from_lanes(jnp.sum(gathered_ref[...], axis=0), 2) * both[1:2]
    return jnp.concatenate([both[0:2], sums, jnp.zeros((5, C), F32)], axis=0)


def in_lanes(row):
    tail = jnp.concatenate([row[:, 256:], jnp.zeros((1, 3 * 128 - C), F32)], axis=1)
    return [row[:, :128], row[:, 128:256], tail]


def from_lanes(sums, at):
    parts = [sums[at : at + 1], sums[at + 1 : at + 2], sums[at + 2 : at + 3, : C - 256]]
    return jnp.concatenate(parts, axis=1)


def own_stats(hidden, mask, first, limit):
    held = jnp.clip(limit - first, 0, F_DEV).astype(F32) * UNIT
    sums = jnp.sum(hidden * mask, axis=0, keepdims=True)
    pad = jnp.zeros_like(sums)
    mean = exact_dot(two_rows(sums, pad), to_groups()) / jnp.maximum(held, 1.0)
    off = hidden - exact_dot(mean, to_channels())[0:1]
    square = jnp.sum(off * off * mask, axis=0, keepdims=True)
    square = exact_dot(two_rows(pad, square), to_groups())
    by_channel = jnp.sum(off * mask, axis=0, keepdims=True)
    rest = [jnp.zeros((3, 128), F32)]
    return jnp.concatenate([mean[0:1], square[1:2]] + in_lanes(by_channel) + rest, axis=0)


def put_stats(stats, out_ref):
    for peer in range(PEERS):
        out_ref[peer] = stats


def put_edges(value, low_ref, high_ref):
    low_ref[...] = value[:PLANE]
    high_ref[...] = value[CELLS - PLANE :]


def conv_kernel(place, x_ref, w_ref, bias_ref, hidden_ref, low_ref, high_ref, stats_ref):
    hidden = conv(x_ref[...].astype(F32), w_ref) + bias_ref[...]
    hidden_ref[...] = hidden
    put_edges(hidden, low_ref, high_ref)
    first, limit = place[0], place[1]
    put_stats(own_stats(hidden, live_mask(first, limit, F_DEV), first, limit), stats_ref)


def activate(place, hidden, moments, gain, frames_before, frames):
    normed = (hidden - moments[0:1]) * moments[1:2]
    scaled = normed * gain
    mask = live_mask(place[0] - frames_before, place[1], frames)
    return (mask * (scaled * jax.nn.sigmoid(scaled))).astype(BF16)


def activate_all(place, before_ref, hidden_ref, after_ref, gathered_ref, gain_ref, act_ref, moments_ref):
    moments = joined_stats(gathered_ref, place[1])
    moments_ref[...] = moments
    gain = gain_ref[...]
    act_ref[:PLANE] = activate(place, before_ref[...], moments, gain, 1, 1)
    act_ref[PLANE : PLANE + CELLS] = activate(place, hidden_ref[...], moments, gain, 0, F_DEV)
    act_ref[PLANE + CELLS :] = activate(place, after_ref[...], moments, gain, -F_DEV, 1)


def section_output(act_ref, x_ref, t_ref):
    wide = jnp.concatenate([act_ref[k * PLANE : k * PLANE + CELLS] for k in range(3)], axis=1)
    temporal = dot(wide, t_ref[...].reshape(3 * C, C))
    return (x_ref[...].astype(F32) + temporal).astype(BF16)


def output_kernel(
    place, before, hidden, after, gathered, gain, x, t, act_ref, moments_ref, out_ref
):
    activate_all(place, before, hidden, after, gathered, gain, act_ref, moments_ref)
    out = section_output(act_ref, x, t).astype(F32).reshape(F_DEV * ROWS, PITCH, C)
    out_ref[...] = out[:, :WIDTH].astype(BF16)


def fetch(place, sources, w_out, t_out, sems, begin):
    w, t, near, near_other, far, far_other, on, on_other = sources
    back, core = place[2], place[3]

    def go(*pairs):
        for n, (source, target) in enumerate(pairs):
            job = pltpu.make_async_copy(source, target, sems.at[n])
            if begin:
                job.start()
            else:
                job.wait()

    @pl.when(back == 0)
    def _():
        go((w, w_out), (t, t_out))

    for d, held in ((1, (near, near_other)), (2, (on, on_other)), (3, (far, far_other))):
        for c in range(2):

            @pl.when((back == d) & (core == c))
            def _(lower=held[c], upper=held[1 - c]):
                go(
                    (lower, w_out.at[pl.ds(0, 6)]),
                    (upper.at[pl.ds(0, 3)], w_out.at[pl.ds(6, 3)]),
                    (upper.at[pl.ds(3, 3)], t_out),
                )


def fetched_conv_kernel(place, x, bias, *rest):
    sources, (hidden_ref, low, high, stats, w_out, t_out) = rest[:8], rest[8:14]
    sems = rest[14]
    fetch(place, sources, w_out, t_out, sems, True)
    fetch(place, sources, w_out, t_out, sems, False)
    conv_kernel(place, x, w_out, bias, hidden_ref, low, high, stats)


def section_kernel(joins, place, before, hidden, after, gathered, gain, x, t, bias, *rest):
    if joins:
        skip, rest = rest[0], rest[1:]
    sources, rest = rest[:8], rest[8:]
    act_ref, moments_ref, out_ref, hidden_ref, low, high, stats_ref, w_out, t_out = rest[:9]
    sems = rest[9]
    fetch(place, sources, w_out, t_out, sems, True)
    activate_all(place, before, hidden, after, gathered, gain, act_ref, moments_ref)
    out = section_output(act_ref, x, t)
    if joins:
        out = (out.astype(F32) + skip[...].astype(F32)).astype(BF16)
    out_ref[...] = out
    fetch(place, sources, w_out, t_out, sems, False)
    conv_kernel(place, out_ref, w_out, bias, hidden_ref, low, high, stats_ref)


def act_grad_kernel(
    mode, place, u_before, u, u_after, *rest
):
    first, limit = place[0], place[1]
    if mode == "last":
        (before, hidden, after, gathered, gain_ref, t, act_ref, moments_ref, grad_ref, sums_ref) = rest
        activate_all(place, before, hidden, after, gathered, gain_ref, act_ref, moments_ref)
        planes = [u_before[...], u[...], u_after[...]]
    elif mode == "first":
        (s_before, s, s_after, hidden, moments_ref, gain_ref, t, u_out, grad_ref, sums_ref) = rest
        planes = [
            (p[...].astype(F32) + q[...].astype(F32)).astype(BF16)
            for p, q in ((u_before, s_before), (u, s), (u_after, s_after))
        ]
        u_out[...] = planes[1]
    else:
        hidden, moments_ref, gain_ref, t, grad_ref, sums_ref = rest
        planes = [u_before[...], u[...], u_after[...]]
    ext = jnp.concatenate(planes, axis=0)
    wide = jnp.concatenate([ext[(2 - k) * PLANE : (2 - k) * PLANE + CELLS] for k in range(3)], axis=1)
    taps = jnp.concatenate([t[0], t[1], t[2]], axis=1)
    act_grad = dot_back(wide, taps)
    gain = gain_ref[...]
    normed = (hidden[...] - moments_ref[0:1]) * moments_ref[1:2]
    scaled = normed * gain
    gate = jax.nn.sigmoid(scaled)
    scaled_grad = act_grad * live_mask(first, limit, F_DEV) * gate * (1.0 + scaled * (1.0 - gate))
    by_normed = jnp.sum(scaled_grad * normed, axis=0, keepdims=True)
    grad = scaled_grad * gain
    grad_ref[...] = grad
    plain = jnp.sum(grad, axis=0, keepdims=True)
    groups = exact_dot(two_rows(plain, by_normed * gain), to_groups())
    rows = [groups[0:2]] + in_lanes(plain) + in_lanes(by_normed)
    put_stats(jnp.concatenate(rows, axis=0), sums_ref)


def hidden_grad(place, grad_ref, hidden_ref, moments_ref, sums_ref, hg_ref, col_ref):
    first, limit = place[0], place[1]
    total = limit.astype(F32) * UNIT
    sums = jnp.sum(sums_ref[...], axis=0)
    means = exact_dot(sums, to_channels()) / total
    normed = (hidden_ref[...] - moments_ref[0:1]) * moments_ref[1:2]
    mask = live_mask(first, limit, F_DEV)
    hg = moments_ref[1:2] * (grad_ref[...] - mask * (means[0:1] + normed * means[1:2]))
    hg = hg.astype(BF16)
    hg_ref[...] = hg
    cells = limit.astype(F32) * (ROWS * WIDTH)
    col = from_lanes(sums, 2) - means[0:1] * cells - means[1:2] * moments_ref[2:3]
    col_ref[...] = two_rows(moments_ref[1:2] * col, from_lanes(sums, 5))
    return hg.astype(F32)


def input_grad_kernel(place, grad, hidden, moments, sums, u, w, hg_ref, col_ref, out_ref, low, high):
    hg = hidden_grad(place, grad, hidden, moments, sums, hg_ref, col_ref)
    out = u[...].astype(F32) + conv_back(hg, w)
    out = (out * col_mask(CELLS)).astype(BF16)
    out_ref[...] = out
    put_edges(out, low, high)


def hidden_grad_kernel(place, grad, hidden, moments, sums, hg_ref, col_ref):
    hidden_grad(place, grad, hidden, moments, sums, hg_ref, col_ref)


ACT = ((CELLS, C), BF16)
HID = ((CELLS, C), F32)
EXT = (((F_DEV + 2) * PLANE, C), BF16)
ROW8 = ((8, C), F32)
STATS = ((PEERS, 8, 128), F32)


EDGE = ((PLANE, C), BF16)
WIDE_EDGE = ((PLANE, C), F32)
CONV_OUT = (HID, WIDE_EDGE, WIDE_EDGE, STATS)
TAPS = (((9, C, C), BF16), ((3, C, C), BF16))


def run(kernel, place, args, outs, sources=()):
    vmem = pl.BlockSpec(memory_space=pltpu.VMEM)
    hbm = pl.BlockSpec(memory_space=pltpu.HBM)
    return pl.pallas_call(
        kernel,
        out_shape=tuple(jax.ShapeDtypeStruct(s, d) for s, d in outs),
        in_specs=[pl.BlockSpec(memory_space=pltpu.SMEM)]
        + [vmem] * len(args)
        + [hbm] * len(sources),
        out_specs=tuple(vmem for _ in outs),
        scratch_shapes=[pltpu.SemaphoreType.DMA((3,))] if sources else [],
        compiler_params=pltpu.CompilerParams(vmem_limit_bytes=VMEM_LIMIT),
    )(place, *args, *sources)


def weight_grad_kernel(place, *refs):
    lists, (keep_ref, give_ref), scratch = refs[:16], refs[16:18], refs[18:]
    bufs, wide_ref, spatial, temporal, chunks, sems = scratch[:4], *scratch[4:]
    segment, core, half = place[0], place[1], place[2]
    for k in range(4):

        @pl.when(segment == k)
        def _(k=k):
            jobs = [
                pltpu.make_async_copy(lists[4 * k + n], bufs[n], sems.at[n]) for n in range(4)
            ]
            for job in jobs:
                job.start()
            for job in jobs:
                job.wait()

    x, hg, act, u = bufs
    wide_ref[...] = shifted_columns(x[...].astype(F32))
    hidden_grad = hg[...]
    gap = jnp.zeros((PITCH, C), BF16)
    spread_grad = jnp.concatenate([hidden_grad[:PLANE], gap, hidden_grad[PLANE:]], axis=0)
    upstream = u[...]
    over_cells = (((0,), (0,)), ((), ()))

    def taps(k, carry):
        rows = wide_ref[pl.ds(pl.multiple_of(k * PITCH, PITCH), SPAN), :]
        spatial[pl.ds(pl.multiple_of(3 * C * k, 8), 3 * C)] = lax.dot_general(
            rows, spread_grad, over_cells, preferred_element_type=F32
        )
        rows = act[pl.ds(pl.multiple_of(k * PLANE, PLANE), CELLS), :]
        temporal[pl.ds(pl.multiple_of(C * k, 8), C)] = lax.dot_general(
            rows, upstream, over_cells, preferred_element_type=F32
        )
        return carry

    lax.fori_loop(0, 3, taps, 0)

    def cut(n, carry):
        rows = spatial[pl.ds(pl.multiple_of(720 * n, 8), 720), :]
        more = temporal[pl.ds(pl.multiple_of(240 * n, 8), 240), :]
        for m in range(8):
            both = []
            for p in (2 * m, 2 * m + 1):
                both += [rows[45 * p : 45 * p + 45], more[15 * p : 15 * p + 15]]
            chunks[8 * n + m] = jnp.concatenate(both, axis=0).astype(BF16)
        return carry

    lax.fori_loop(0, 4, cut, 0)
    for q in range(PEERS // 2):
        keep_ref[q] = chunks[4 * q + 2 * core + half]
        give_ref[q, :, :C] = chunks[4 * q + 2 * (1 - core) + half]
        give_ref[q, :, C:] = jnp.zeros((120, PADDED - C), BF16)


def weight_grads(place, kept):
    hbm = pl.BlockSpec(memory_space=pltpu.HBM)
    vmem = pl.BlockSpec(memory_space=pltpu.VMEM)
    lists = [state[name] for state in kept for name in ("x", "hg", "act", "u")]
    chunks = [jax.ShapeDtypeStruct((PEERS // 2, 120, c), BF16) for c in (C, PADDED)]
    return pl.pallas_call(
        weight_grad_kernel,
        out_shape=tuple(chunks),
        in_specs=[pl.BlockSpec(memory_space=pltpu.SMEM)] + [hbm] * 16,
        out_specs=(vmem, vmem),
        scratch_shapes=[
            pltpu.VMEM((CELLS, C), BF16),
            pltpu.VMEM((CELLS, C), BF16),
            pltpu.VMEM(((F_DEV + 2) * PLANE, C), BF16),
            pltpu.VMEM((CELLS, C), BF16),
            pltpu.VMEM((SPAN + 2 * PITCH, 3 * C), BF16),
            pltpu.VMEM((9 * C, C), F32),
            pltpu.VMEM((3 * C, C), F32),
            pltpu.VMEM((2 * PEERS, 120, C), BF16),
            pltpu.SemaphoreType.DMA((4,)),
        ],
        name="weight_grads",
        compiler_params=pltpu.CompilerParams(vmem_limit_bytes=56 * 1024 * 1024),
    )(place, *lists)


def core_sum_kernel(place, keep, got, mine, theirs):
    for q in range(PEERS // 2):
        total = keep[q].astype(F32) + got[q, :, :C].astype(F32)
        low, high = total[:60], total[60:]
        first = place[3] == 0
        mine[q] = jnp.where(first, low, high).astype(BF16)
        theirs[q] = jnp.where(first, high, low).astype(BF16)


def row_sum_kernel(place, mine, got, out):
    for q in range(PEERS // 2):
        out[q] = (mine[q].astype(F32) + got[q].astype(F32)).astype(BF16)


def frame_sum_kernel(place, got, spatial, temporal):
    total = got[0].astype(F32)
    for q in range(1, PEERS // 2):
        total = total + got[q].astype(F32)
    spatial[...] = total[:45]
    temporal[...] = total[45:]


def time_features(timesteps):
    half_dim = TE // 2
    frequency = jnp.exp(-jnp.log(10000.0) * jnp.arange(half_dim).astype(jnp.float32) / half_dim)
    angles = timesteps.astype(jnp.float32)[:, None] * frequency[None, :]
    wave_parts = jnp.concatenate([jnp.cos(angles), jnp.sin(angles)], axis=1)
    return jax.nn.silu(wave_parts).astype(jnp.bfloat16)


def for_each_row(arrays):
    rows = lax.axis_size("row")
    return jnp.stack([jnp.stack([array[r % CLIPS] for array in arrays]) for r in range(rows)])


def whole_frames(got):
    got = jnp.transpose(got, (1, 2, 0, 3, 4, 5)).reshape(-1, F_DEV, ROWS, WIDTH, C)
    got = jnp.pad(got, ((0, 0), (0, 0), (0, 0), (0, PITCH - WIDTH), (0, 0)))
    return [part.reshape(CELLS, C) for part in got]


def exchange(stats):
    return lax.all_to_all(stats, "frame", 0, 0)


def halo(low, high):
    up = [(i, i + 1) for i in range(PEERS - 1)]
    before = lax.ppermute(high, "frame", up)
    after = lax.ppermute(low, "frame", [(j, i) for i, j in up])
    return before, after


def from_segment_zero(array, segment_index, sections):
    got = [lax.ppermute(array, "segment", [(0, j)]) for j in range(1, sections)]
    return jnp.where(segment_index == 0, array, sum(got[1:], got[0]))


def pick(options, segment_index):
    out = options[0]
    for k in range(1, len(options)):
        out = jnp.where(segment_index == k, options[k], out)
    return out


def per_device(
    latents,
    cotangent,
    timesteps,
    frame_counts,
    spatial_weight,
    temporal_weight,
    time_weight,
    norm_gain,
):
    sections = lax.axis_size("segment")
    segment_index = lax.axis_index("segment")
    frame_index = lax.axis_index("frame")
    row_index = lax.axis_index("row")
    clip = row_index % CLIPS
    core = frame_index % 2
    kernel = spatial_weight[0]
    tkernel = temporal_weight[0]

    limit = lax.dynamic_index_in_dim(frame_counts, clip, 0, keepdims=False)
    first = frame_index * F_DEV

    def place_of(k):
        back = (segment_index - k) % sections
        return jnp.stack([first, limit, back, core]).astype(jnp.int32)


    cells = for_each_row((latents, cotangent))
    cells, kernel, tkernel = lax.optimization_barrier((cells, kernel, tkernel))
    half = jnp.where(core == 0, kernel[:6], jnp.concatenate([kernel[6:], tkernel], axis=0))
    cells = lax.all_to_all(cells, "row", 0, 0)
    near = lax.ppermute(half, "segment", [(1, 2), (2, 3), (3, 0)])
    far = lax.ppermute(half, "segment", [(1, 0), (2, 1), (3, 2)])
    x, cot = whole_frames(cells)
    swap = [(i, i ^ 1) for i in range(PEERS)]

    time_embed = time_features(timesteps)
    biases = jnp.dot(time_embed, time_weight[0], preferred_element_type=jnp.float32)
    own_rows = jnp.concatenate([biases, norm_gain, jnp.zeros((5, C), F32)], axis=0)
    own_bias = jnp.where(clip == 0, biases[0:1], biases[1:2])


    used = jnp.repeat(first + jnp.arange(F_DEV) < limit, PLANE)
    places = [place_of(k) for k in range(sections)]
    side_place = jnp.stack([segment_index, core, row_index // 2, row_index % 2]).astype(jnp.int32)
    x, own_bias, own_rows, used, places, side_place = lax.optimization_barrier(
        (x, own_bias, own_rows, used, places, side_place)
    )
    place = places[0]

    hidden, low, high, stats = run(conv_kernel, place, (x, kernel, own_bias), CONV_OUT)
    before, after = halo(low, high)
    gathered = exchange(stats)
    gathered, near, far = lax.optimization_barrier((gathered, near, far))

    def onward(up, down):
        return [(s * PEERS + f, t * PEERS + f) for s, t in up for f in range(0, PEERS, 2)] + [
            (s * PEERS + f, t * PEERS + f) for s, t in down for f in range(1, PEERS, 2)
        ]

    passed = jnp.where(core == 0, near, far)
    gathered, passed = lax.optimization_barrier((gathered, passed))
    everyone = ("segment", "frame")
    on = lax.ppermute(passed, everyone, onward([(2, 3), (3, 0)], [(0, 3), (1, 0)]))
    act, moments, out = run(
        output_kernel,
        place,
        (before, hidden, after, gathered, norm_gain, x, tkernel),
        (EXT, ROW8, ((F_DEV * ROWS, WIDTH, C), BF16)),
    )
    kept = [dict(x=x, hidden=hidden, act=act, moments=moments)]
    out, near, far, cot, own_rows = lax.optimization_barrier((out, near, far, cot, own_rows))
    rows_from = [own_rows]
    x = from_segment_zero(out, segment_index, sections)
    for d in range(1, sections):
        pairs = [(k, (k + d) % sections) for k in range(sections)]
        rows_from.append(lax.ppermute(own_rows, "segment", pairs))
    near_other = lax.ppermute(near, "frame", swap)
    far_other = lax.ppermute(far, "frame", swap)

    def rows_of(k):
        rows = pick(rows_from, (segment_index - k) % sections)
        bias = jnp.where(clip == 0, rows[0:1], rows[1:2])
        return bias, rows[2:3]

    cot = jnp.where(used[:, None], cot, jnp.zeros_like(cot))
    sides = halo(cot[:PLANE], cot[CELLS - PLANE :])
    small = [rows_of(k) + (places[k],) for k in range(1, sections)]
    x = jnp.pad(x, ((0, 0), (0, PITCH - WIDTH), (0, 0))).reshape(CELLS, C)
    x, on, cot, sides, small, passed = lax.optimization_barrier((x, on, cot, sides, small, passed))
    cot_before, cot_after = sides
    on_other = lax.ppermute(on, "frame", swap)
    last = lax.ppermute(passed, everyone, onward([(0, 1)], [(2, 1)]))
    fetched = (kernel, tkernel, near, near_other, far, far_other)
    sources = fetched + (on, on_other)

    skip = x
    weights = [(kernel, tkernel)]
    gains = [norm_gain]
    for k in range(1, sections):
        bias, gain, its_place = small[k - 1]
        gains.append(gain)
        if k == 1:
            hidden, low, high, stats, *taps = run(
                fetched_conv_kernel, its_place, (x, bias), CONV_OUT + TAPS, sources
            )
        else:
            joins = k == sections - 1
            args = (before, hidden, after, gathered, gains[k - 1], x, weights[k - 1][1], bias)
            args += (skip,) if joins else ()
            act, moments, x, hidden, low, high, stats, *taps = run(
                functools.partial(section_kernel, joins),
                its_place,
                args,
                (EXT, ROW8, ACT) + CONV_OUT + TAPS,
                sources,
            )
            kept[k - 1].update(act=act, moments=moments)
        weights.append(taps)
        kept.append(dict(x=x, hidden=hidden))
        if k == 2:
            low, last = lax.optimization_barrier((low, last))
        before, after = halo(low, high)
        gathered = exchange(stats)
        if k == 2:
            last_other = lax.ppermute(last, "frame", swap)
            sources = fetched + (last, last_other)

    u, u_before, u_after = cot, cot_before, cot_after
    skip_u = None
    for k in reversed(range(sections)):
        state = kept[k]
        sides = (u_before, u, u_after)
        if k == sections - 1:
            act, moments, grad, sums = run(
                functools.partial(act_grad_kernel, "last"),
                place,
                sides + (before, state["hidden"], after, gathered, gains[k], weights[k][1]),
                (EXT, ROW8, HID, STATS),
            )
            state.update(act=act, moments=moments)
        elif k == 0:
            u, grad, sums = run(
                functools.partial(act_grad_kernel, "first"),
                place,
                sides + skip_u + (state["hidden"], state["moments"], gains[k], weights[k][1]),
                (ACT, HID, STATS),
            )
        else:
            grad, sums = run(
                functools.partial(act_grad_kernel, "mid"),
                place,
                sides + (state["hidden"], state["moments"], gains[k], weights[k][1]),
                (HID, STATS),
            )
        state.update(u=u)
        sums = exchange(sums)
        args = (grad, state["hidden"], state["moments"], sums)
        if k > 0:
            hg, col, u, low, high = run(
                input_grad_kernel, place, args + (u, weights[k][0]), (ACT, ROW8, ACT, EDGE, EDGE)
            )
            u_before, u_after = halo(low, high)
            if k == sections - 1:
                skip_u = (u_before, u, u_after)
        else:
            hg, col = run(hidden_grad_kernel, place, args, (ACT, ROW8))
        state.update(hg=hg, col=col)

    partner = [(i, i ^ 1) for i in range(4)]
    keep, give = weight_grads(side_place, kept)
    got = lax.ppermute(give, "frame", swap)
    col = pick([state["col"] for state in kept], segment_index)
    other = lax.ppermute(col, "row", partner)
    chunk = ((PEERS // 2, 60, C), BF16)
    keep, give = run(core_sum_kernel, side_place, (keep, got), (chunk, chunk))
    got = lax.ppermute(give, "row", partner)
    (summed,) = run(row_sum_kernel, side_place, (keep, got), (chunk,))
    groups = [[i for i in range(PEERS) if i % 2 == c] for c in range(2)]
    got = lax.all_to_all(summed, "frame", 0, 0, axis_index_groups=groups)
    spatial_out, temporal_out = run(
        frame_sum_kernel, side_place, (got,), (((45, C), F32), ((15, C), F32))
    )

    peers = 4 * PEERS
    gain_total = col[1] + other[1]
    totals = [jnp.where(clip == c, col[0], other[0]) for c in range(CLIPS)]
    spot = frame_index * 4 + row_index
    gain_out = lax.dynamic_slice_in_dim(gain_total, spot * (C // peers), C // peers)
    features = lax.dynamic_slice_in_dim(time_embed, spot * (TE // peers), TE // peers, axis=1)
    features = features.astype(F32)
    time_out = sum(features[c][:, None] * totals[c][None, :] for c in range(CLIPS))
    return (spatial_out[None], temporal_out[None], time_out[None], gain_out[None])


def solution(mesh):
    return jax.shard_map(
        per_device,
        mesh=mesh,
        in_specs=(
            P(None, "frame", "row", None, None),
            P(None, "frame", "row", None, None),
            P(),
            P(),
            P("segment", None, None, None),
            P("segment", None, None, None),
            P("segment", None, None),
            P("segment", None),
        ),
        out_specs=(
            P("segment", ("frame", "row"), None),
            P("segment", ("frame", "row"), None),
            P("segment", ("frame", "row"), None),
            P("segment", ("frame", "row")),
        ),
        check_vma=False,
    )
```

```python
import functools

import jax
import jax.numpy as jnp
from jax import lax
from jax.experimental import pallas as pl
from jax.experimental.pallas import tpu as pltpu
from jax.sharding import PartitionSpec as P


C = 320
G = 32
TE = 1280
WIDTH = 24
PITCH = 32
ROWS = 8
F_DEV = 2
CLIPS = 2
EPSILON = 1e-05

PLANE = ROWS * PITCH
CELLS = F_DEV * PLANE
UNIT = float(ROWS * WIDTH * (C // G))
PEERS = 16
PADDED = 384
VMEM_LIMIT = 20 * 1024 * 1024
F32 = jnp.float32
BF16 = jnp.bfloat16


def dot(a, b):
    return jnp.dot(a, b, preferred_element_type=F32)


def dot_back(a, b):
    return lax.dot_general(a, b, (((1,), (1,)), ((), ())), preferred_element_type=F32)


def exact_dot(a, b):
    return jnp.dot(a, b, preferred_element_type=F32, precision=lax.Precision.HIGHEST)


def to_groups():
    ch = lax.broadcasted_iota(jnp.int32, (C, 128), 0)
    low = lax.broadcasted_iota(jnp.int32, (C, 128), 1) * (C // G)
    return ((ch >= low) & (ch < low + C // G)).astype(F32)


def to_channels():
    ch = lax.broadcasted_iota(jnp.int32, (128, C), 1)
    low = lax.broadcasted_iota(jnp.int32, (128, C), 0) * (C // G)
    return ((ch >= low) & (ch < low + C // G)).astype(F32)


def col_mask(rows):
    at = lax.broadcasted_iota(jnp.int32, (rows, 1), 0)
    return (jnp.bitwise_and(at, PITCH - 1) < WIDTH).astype(F32)


def live_mask(first, limit, frames):
    parts = []
    for f in range(frames):
        ok = jnp.where((first + f >= 0) & (first + f < limit), 1.0, 0.0)
        parts.append(jnp.full((PLANE, 1), 1.0, F32) * ok)
    return jnp.concatenate(parts, axis=0) * col_mask(frames * PLANE)


def two_rows(top, second):
    return jnp.concatenate([top, second, jnp.zeros((6, top.shape[1]), F32)], axis=0)


def shifted_columns(x):
    rows = x.shape[0]
    gap = jnp.zeros((PITCH, 3 * C), BF16)
    wide = jnp.concatenate(
        [
            pltpu.roll(x, 1, 0).astype(BF16),
            x.astype(BF16),
            pltpu.roll(x, rows - 1, 0).astype(BF16),
        ],
        axis=1,
    )
    return jnp.concatenate([gap, wide[:PLANE], gap, wide[PLANE:], gap], axis=0)


SPAN = CELLS + PITCH


def without_gap(x):
    return jnp.concatenate([x[:PLANE], x[PLANE + PITCH :]], axis=0)


def conv(x, w_ref):
    wide = shifted_columns(x)
    total = None
    for a in range(3):
        taps = w_ref[3 * a : 3 * a + 3].reshape(3 * C, C)
        part = dot(wide[a * PITCH : a * PITCH + SPAN], taps)
        total = part if total is None else total + part
    return without_gap(total)


def conv_back(x, w_ref):
    wide = shifted_columns(x)
    total = None
    for a in range(3):
        taps = jnp.concatenate([w_ref[3 * a + 2], w_ref[3 * a + 1], w_ref[3 * a]], axis=1)
        part = dot_back(wide[(2 - a) * PITCH : (2 - a) * PITCH + SPAN], taps)
        total = part if total is None else total + part
    return without_gap(total)


def joined_stats(gathered_ref, limit):
    means = gathered_ref[:, 0, :]
    squares = gathered_ref[:, 1, :]
    peer = lax.broadcasted_iota(jnp.int32, (PEERS, 128), 0)
    held = jnp.clip(limit - peer * F_DEV, 0, F_DEV).astype(F32) * UNIT
    total = limit.astype(F32) * UNIT
    mean = jnp.sum(held * means, axis=0, keepdims=True) / total
    apart = means - mean
    variance = jnp.sum(squares + held * apart * apart, axis=0, keepdims=True) / total
    both = exact_dot(two_rows(mean, lax.rsqrt(variance + EPSILON)), to_channels())
    sums = from_lanes(jnp.sum(gathered_ref[...], axis=0), 2) * both[1:2]
    return jnp.concatenate([both[0:2], sums, jnp.zeros((5, C), F32)], axis=0)


def in_lanes(row):
    tail = jnp.concatenate([row[:, 256:], jnp.zeros((1, 3 * 128 - C), F32)], axis=1)
    return [row[:, :128], row[:, 128:256], tail]


def from_lanes(sums, at):
    parts = [sums[at : at + 1], sums[at + 1 : at + 2], sums[at + 2 : at + 3, : C - 256]]
    return jnp.concatenate(parts, axis=1)


def own_stats(hidden, mask, first, limit):
    held = jnp.clip(limit - first, 0, F_DEV).astype(F32) * UNIT
    sums = jnp.sum(hidden * mask, axis=0, keepdims=True)
    pad = jnp.zeros_like(sums)
    mean = exact_dot(two_rows(sums, pad), to_groups()) / jnp.maximum(held, 1.0)
    off = hidden - exact_dot(mean, to_channels())[0:1]
    square = jnp.sum(off * off * mask, axis=0, keepdims=True)
    square = exact_dot(two_rows(pad, square), to_groups())
    by_channel = jnp.sum(off * mask, axis=0, keepdims=True)
    rest = [jnp.zeros((3, 128), F32)]
    return jnp.concatenate([mean[0:1], square[1:2]] + in_lanes(by_channel) + rest, axis=0)


def put_stats(stats, out_ref):
    for peer in range(PEERS):
        out_ref[peer] = stats


def put_edges(value, low_ref, high_ref):
    low_ref[...] = value[:PLANE]
    high_ref[...] = value[CELLS - PLANE :]


def conv_kernel(place, x_ref, w_ref, bias_ref, hidden_ref, low_ref, high_ref, stats_ref):
    hidden = conv(x_ref[...].astype(F32), w_ref) + bias_ref[...]
    hidden_ref[...] = hidden
    put_edges(hidden, low_ref, high_ref)
    first, limit = place[0], place[1]
    put_stats(own_stats(hidden, live_mask(first, limit, F_DEV), first, limit), stats_ref)


def activate(place, hidden, moments, gain, frames_before, frames):
    normed = (hidden - moments[0:1]) * moments[1:2]
    scaled = normed * gain
    mask = live_mask(place[0] - frames_before, place[1], frames)
    return (mask * (scaled * jax.nn.sigmoid(scaled))).astype(BF16)


def activate_all(place, before_ref, hidden_ref, after_ref, gathered_ref, gain_ref, act_ref, moments_ref):
    moments = joined_stats(gathered_ref, place[1])
    moments_ref[...] = moments
    gain = gain_ref[...]
    act_ref[:PLANE] = activate(place, before_ref[...], moments, gain, 1, 1)
    act_ref[PLANE : PLANE + CELLS] = activate(place, hidden_ref[...], moments, gain, 0, F_DEV)
    act_ref[PLANE + CELLS :] = activate(place, after_ref[...], moments, gain, -F_DEV, 1)


def section_output(act_ref, x_ref, t_ref):
    wide = jnp.concatenate([act_ref[k * PLANE : k * PLANE + CELLS] for k in range(3)], axis=1)
    temporal = dot(wide, t_ref[...].reshape(3 * C, C))
    return (x_ref[...].astype(F32) + temporal).astype(BF16)


def output_kernel(
    place, before, hidden, after, gathered, gain, x, t, act_ref, moments_ref, out_ref
):
    activate_all(place, before, hidden, after, gathered, gain, act_ref, moments_ref)
    out = section_output(act_ref, x, t).astype(F32).reshape(F_DEV * ROWS, PITCH, C)
    out_ref[...] = out[:, :WIDTH].astype(BF16)


def fetch(place, sources, w_out, t_out, sems, begin):
    w, t, near, near_other, far, far_other, on, on_other = sources
    back, core = place[2], place[3]

    def go(*pairs):
        for n, (source, target) in enumerate(pairs):
            job = pltpu.make_async_copy(source, target, sems.at[n])
            if begin:
                job.start()
            else:
                job.wait()

    @pl.when(back == 0)
    def _():
        go((w, w_out), (t, t_out))

    for d, held in ((1, (near, near_other)), (2, (on, on_other)), (3, (far, far_other))):
        for c in range(2):

            @pl.when((back == d) & (core == c))
            def _(lower=held[c], upper=held[1 - c]):
                go(
                    (lower, w_out.at[pl.ds(0, 6)]),
                    (upper.at[pl.ds(0, 3)], w_out.at[pl.ds(6, 3)]),
                    (upper.at[pl.ds(3, 3)], t_out),
                )


def fetched_conv_kernel(place, x, bias, *rest):
    sources, (hidden_ref, low, high, stats, w_out, t_out) = rest[:8], rest[8:14]
    sems = rest[14]
    fetch(place, sources, w_out, t_out, sems, True)
    fetch(place, sources, w_out, t_out, sems, False)
    conv_kernel(place, x, w_out, bias, hidden_ref, low, high, stats)


def section_kernel(joins, place, before, hidden, after, gathered, gain, x, t, bias, *rest):
    if joins:
        skip, rest = rest[0], rest[1:]
    sources, rest = rest[:8], rest[8:]
    act_ref, moments_ref, out_ref, hidden_ref, low, high, stats_ref, w_out, t_out = rest[:9]
    sems = rest[9]
    fetch(place, sources, w_out, t_out, sems, True)
    activate_all(place, before, hidden, after, gathered, gain, act_ref, moments_ref)
    out = section_output(act_ref, x, t)
    if joins:
        out = (out.astype(F32) + skip[...].astype(F32)).astype(BF16)
    out_ref[...] = out
    fetch(place, sources, w_out, t_out, sems, False)
    conv_kernel(place, out_ref, w_out, bias, hidden_ref, low, high, stats_ref)


def act_grad_kernel(
    mode, place, u_before, u, u_after, *rest
):
    first, limit = place[0], place[1]
    if mode == "last":
        (before, hidden, after, gathered, gain_ref, t, act_ref, moments_ref, grad_ref, sums_ref) = rest
        activate_all(place, before, hidden, after, gathered, gain_ref, act_ref, moments_ref)
        planes = [u_before[...], u[...], u_after[...]]
    elif mode == "first":
        (s_before, s, s_after, hidden, moments_ref, gain_ref, t, u_out, grad_ref, sums_ref) = rest
        planes = [
            (p[...].astype(F32) + q[...].astype(F32)).astype(BF16)
            for p, q in ((u_before, s_before), (u, s), (u_after, s_after))
        ]
        u_out[...] = planes[1]
    else:
        hidden, moments_ref, gain_ref, t, grad_ref, sums_ref = rest
        planes = [u_before[...], u[...], u_after[...]]
    ext = jnp.concatenate(planes, axis=0)
    wide = jnp.concatenate([ext[(2 - k) * PLANE : (2 - k) * PLANE + CELLS] for k in range(3)], axis=1)
    taps = jnp.concatenate([t[0], t[1], t[2]], axis=1)
    act_grad = dot_back(wide, taps)
    gain = gain_ref[...]
    normed = (hidden[...] - moments_ref[0:1]) * moments_ref[1:2]
    scaled = normed * gain
    gate = jax.nn.sigmoid(scaled)
    scaled_grad = act_grad * live_mask(first, limit, F_DEV) * gate * (1.0 + scaled * (1.0 - gate))
    by_normed = jnp.sum(scaled_grad * normed, axis=0, keepdims=True)
    grad = scaled_grad * gain
    grad_ref[...] = grad
    plain = jnp.sum(grad, axis=0, keepdims=True)
    groups = exact_dot(two_rows(plain, by_normed * gain), to_groups())
    rows = [groups[0:2]] + in_lanes(plain) + in_lanes(by_normed)
    put_stats(jnp.concatenate(rows, axis=0), sums_ref)


def hidden_grad(place, grad_ref, hidden_ref, moments_ref, sums_ref, hg_ref, col_ref):
    first, limit = place[0], place[1]
    total = limit.astype(F32) * UNIT
    sums = jnp.sum(sums_ref[...], axis=0)
    means = exact_dot(sums, to_channels()) / total
    normed = (hidden_ref[...] - moments_ref[0:1]) * moments_ref[1:2]
    mask = live_mask(first, limit, F_DEV)
    hg = moments_ref[1:2] * (grad_ref[...] - mask * (means[0:1] + normed * means[1:2]))
    hg = hg.astype(BF16)
    hg_ref[...] = hg
    cells = limit.astype(F32) * (ROWS * WIDTH)
    col = from_lanes(sums, 2) - means[0:1] * cells - means[1:2] * moments_ref[2:3]
    col_ref[...] = two_rows(moments_ref[1:2] * col, from_lanes(sums, 5))
    return hg.astype(F32)


def input_grad_kernel(place, grad, hidden, moments, sums, u, w, hg_ref, col_ref, out_ref, low, high):
    hg = hidden_grad(place, grad, hidden, moments, sums, hg_ref, col_ref)
    out = u[...].astype(F32) + conv_back(hg, w)
    out = (out * col_mask(CELLS)).astype(BF16)
    out_ref[...] = out
    put_edges(out, low, high)


def hidden_grad_kernel(place, grad, hidden, moments, sums, hg_ref, col_ref):
    hidden_grad(place, grad, hidden, moments, sums, hg_ref, col_ref)


ACT = ((CELLS, C), BF16)
HID = ((CELLS, C), F32)
EXT = (((F_DEV + 2) * PLANE, C), BF16)
ROW8 = ((8, C), F32)
STATS = ((PEERS, 8, 128), F32)


EDGE = ((PLANE, C), BF16)
WIDE_EDGE = ((PLANE, C), F32)
CONV_OUT = (HID, WIDE_EDGE, WIDE_EDGE, STATS)
TAPS = (((9, C, C), BF16), ((3, C, C), BF16))


def run(kernel, place, args, outs, sources=()):
    vmem = pl.BlockSpec(memory_space=pltpu.VMEM)
    hbm = pl.BlockSpec(memory_space=pltpu.HBM)
    return pl.pallas_call(
        kernel,
        out_shape=tuple(jax.ShapeDtypeStruct(s, d) for s, d in outs),
        in_specs=[pl.BlockSpec(memory_space=pltpu.SMEM)]
        + [vmem] * len(args)
        + [hbm] * len(sources),
        out_specs=tuple(vmem for _ in outs),
        scratch_shapes=[pltpu.SemaphoreType.DMA((3,))] if sources else [],
        compiler_params=pltpu.CompilerParams(vmem_limit_bytes=VMEM_LIMIT),
    )(place, *args, *sources)


def weight_grad_kernel(place, *refs):
    lists, (keep_ref, give_ref), scratch = refs[:16], refs[16:18], refs[18:]
    bufs, wide_ref, spatial, temporal, chunks, sems = scratch[:4], *scratch[4:]
    segment, core, half = place[0], place[1], place[2]
    for k in range(4):

        @pl.when(segment == k)
        def _(k=k):
            jobs = [
                pltpu.make_async_copy(lists[4 * k + n], bufs[n], sems.at[n]) for n in range(4)
            ]
            for job in jobs:
                job.start()
            for job in jobs:
                job.wait()

    x, hg, act, u = bufs
    wide_ref[...] = shifted_columns(x[...].astype(F32))
    hidden_grad = hg[...]
    gap = jnp.zeros((PITCH, C), BF16)
    spread_grad = jnp.concatenate([hidden_grad[:PLANE], gap, hidden_grad[PLANE:]], axis=0)
    upstream = u[...]
    over_cells = (((0,), (0,)), ((), ()))

    def taps(k, carry):
        rows = wide_ref[k * PITCH : k * PITCH + SPAN, :]
        spatial[3 * C * k : 3 * C * (k + 1)] = lax.dot_general(
            rows, spread_grad, over_cells, preferred_element_type=F32
        )
        rows = act[k * PLANE : k * PLANE + CELLS, :]
        temporal[C * k : C * (k + 1)] = lax.dot_general(
            rows, upstream, over_cells, preferred_element_type=F32
        )
        return carry

    for k in range(3):
        taps(k, 0)

    def cut(n, carry):
        rows = spatial[pl.ds(pl.multiple_of(720 * n, 8), 720), :]
        more = temporal[pl.ds(pl.multiple_of(240 * n, 8), 240), :]
        for m in range(8):
            both = []
            for p in (2 * m, 2 * m + 1):
                both += [rows[45 * p : 45 * p + 45], more[15 * p : 15 * p + 15]]
            chunks[8 * n + m] = jnp.concatenate(both, axis=0).astype(BF16)
        return carry

    lax.fori_loop(0, 4, cut, 0)
    for q in range(PEERS // 2):
        keep_ref[q] = chunks[4 * q + 2 * core + half]
        give_ref[q, :, :C] = chunks[4 * q + 2 * (1 - core) + half]
        give_ref[q, :, C:] = jnp.zeros((120, PADDED - C), BF16)


def weight_grads(place, kept):
    hbm = pl.BlockSpec(memory_space=pltpu.HBM)
    vmem = pl.BlockSpec(memory_space=pltpu.VMEM)
    lists = [state[name] for state in kept for name in ("x", "hg", "act", "u")]
    chunks = [jax.ShapeDtypeStruct((PEERS // 2, 120, c), BF16) for c in (C, PADDED)]
    return pl.pallas_call(
        weight_grad_kernel,
        out_shape=tuple(chunks),
        in_specs=[pl.BlockSpec(memory_space=pltpu.SMEM)] + [hbm] * 16,
        out_specs=(vmem, vmem),
        scratch_shapes=[
            pltpu.VMEM((CELLS, C), BF16),
            pltpu.VMEM((CELLS, C), BF16),
            pltpu.VMEM(((F_DEV + 2) * PLANE, C), BF16),
            pltpu.VMEM((CELLS, C), BF16),
            pltpu.VMEM((SPAN + 2 * PITCH, 3 * C), BF16),
            pltpu.VMEM((9 * C, C), F32),
            pltpu.VMEM((3 * C, C), F32),
            pltpu.VMEM((2 * PEERS, 120, C), BF16),
            pltpu.SemaphoreType.DMA((4,)),
        ],
        name="weight_grads",
        compiler_params=pltpu.CompilerParams(vmem_limit_bytes=56 * 1024 * 1024),
    )(place, *lists)


def packed(x):
    tail = jnp.concatenate([x[:30, 256:], x[30:, 256:]], axis=1)
    return jnp.concatenate([x[:, :128], x[:, 128:256], tail], axis=0)


def unpacked(x):
    tail = jnp.concatenate([x[120:, :64], x[120:, 64:]], axis=0)
    return jnp.concatenate([x[:60], x[60:120], tail], axis=1)


def core_sum_kernel(place, keep, got, mine, theirs):
    for q in range(PEERS // 2):
        total = keep[q].astype(F32) + got[q, :, :C].astype(F32)
        low, high = packed(total[:60]), packed(total[60:])
        first = place[3] == 0
        mine[q] = jnp.where(first, low, high).astype(BF16)
        theirs[q] = jnp.where(first, high, low).astype(BF16)


def row_sum_kernel(place, mine, got, out):
    for q in range(PEERS // 2):
        out[q] = (mine[q].astype(F32) + got[q].astype(F32)).astype(BF16)


def frame_sum_kernel(place, got, spatial, temporal):
    total = got[0].astype(F32)
    for q in range(1, PEERS // 2):
        total = total + got[q].astype(F32)
    total = unpacked(total)
    spatial[...] = total[:45]
    temporal[...] = total[45:]


def time_features(timesteps):
    half_dim = TE // 2
    frequency = jnp.exp(-jnp.log(10000.0) * jnp.arange(half_dim).astype(jnp.float32) / half_dim)
    angles = timesteps.astype(jnp.float32)[:, None] * frequency[None, :]
    wave_parts = jnp.concatenate([jnp.cos(angles), jnp.sin(angles)], axis=1)
    return jax.nn.silu(wave_parts).astype(jnp.bfloat16)


def for_each_row(arrays):
    rows = lax.axis_size("row")
    return jnp.stack([jnp.stack([array[r % CLIPS] for array in arrays]) for r in range(rows)])


def whole_frames(got):
    got = jnp.transpose(got, (1, 2, 0, 3, 4, 5)).reshape(-1, F_DEV, ROWS, WIDTH, C)
    got = jnp.pad(got, ((0, 0), (0, 0), (0, 0), (0, PITCH - WIDTH), (0, 0)))
    return [part.reshape(CELLS, C) for part in got]


def exchange(stats):
    return lax.all_to_all(stats, "frame", 0, 0)


def halo(low, high):
    up = [(i, i + 1) for i in range(PEERS - 1)]
    before = lax.ppermute(high, "frame", up)
    after = lax.ppermute(low, "frame", [(j, i) for i, j in up])
    return before, after


def from_segment_zero(array, segment_index, sections):
    got = [lax.ppermute(array, "segment", [(0, j)]) for j in range(1, sections)]
    return jnp.where(segment_index == 0, array, sum(got[1:], got[0]))


def pick(options, segment_index):
    out = options[0]
    for k in range(1, len(options)):
        out = jnp.where(segment_index == k, options[k], out)
    return out


def per_device(
    latents,
    cotangent,
    timesteps,
    frame_counts,
    spatial_weight,
    temporal_weight,
    time_weight,
    norm_gain,
):
    sections = lax.axis_size("segment")
    segment_index = lax.axis_index("segment")
    frame_index = lax.axis_index("frame")
    row_index = lax.axis_index("row")
    clip = row_index % CLIPS
    core = frame_index % 2
    kernel = spatial_weight[0]
    tkernel = temporal_weight[0]

    limit = lax.dynamic_index_in_dim(frame_counts, clip, 0, keepdims=False)
    first = frame_index * F_DEV

    def place_of(k):
        back = (segment_index - k) % sections
        return jnp.stack([first, limit, back, core]).astype(jnp.int32)


    cells = for_each_row((latents, cotangent))
    cells, kernel, tkernel = lax.optimization_barrier((cells, kernel, tkernel))
    half = jnp.where(core == 0, kernel[:6], jnp.concatenate([kernel[6:], tkernel], axis=0))
    cells = lax.all_to_all(cells, "row", 0, 0)
    near = lax.ppermute(half, "segment", [(1, 2), (2, 3), (3, 0)])
    far = lax.ppermute(half, "segment", [(1, 0), (2, 1), (3, 2)])
    x, cot = whole_frames(cells)
    swap = [(i, i ^ 1) for i in range(PEERS)]

    time_embed = time_features(timesteps)
    biases = jnp.dot(time_embed, time_weight[0], preferred_element_type=jnp.float32)
    own_rows = jnp.concatenate([biases, norm_gain, jnp.zeros((5, C), F32)], axis=0)
    own_bias = jnp.where(clip == 0, biases[0:1], biases[1:2])


    used = jnp.repeat(first + jnp.arange(F_DEV) < limit, PLANE)
    places = [place_of(k) for k in range(sections)]
    side_place = jnp.stack([segment_index, core, row_index // 2, row_index % 2]).astype(jnp.int32)
    x, own_bias, own_rows, used, places, side_place = lax.optimization_barrier(
        (x, own_bias, own_rows, used, places, side_place)
    )
    place = places[0]

    hidden, low, high, stats = run(conv_kernel, place, (x, kernel, own_bias), CONV_OUT)
    before, after = halo(low, high)
    gathered = exchange(stats)
    gathered, near, far = lax.optimization_barrier((gathered, near, far))

    def onward(up, down):
        return [(s * PEERS + f, t * PEERS + f) for s, t in up for f in range(0, PEERS, 2)] + [
            (s * PEERS + f, t * PEERS + f) for s, t in down for f in range(1, PEERS, 2)
        ]

    passed = jnp.where(core == 0, near, far)
    gathered, passed = lax.optimization_barrier((gathered, passed))
    everyone = ("segment", "frame")
    on = lax.ppermute(passed, everyone, onward([(2, 3), (3, 0)], [(0, 3), (1, 0)]))
    act, moments, out = run(
        output_kernel,
        place,
        (before, hidden, after, gathered, norm_gain, x, tkernel),
        (EXT, ROW8, ((F_DEV * ROWS, WIDTH, C), BF16)),
    )
    kept = [dict(x=x, hidden=hidden, act=act, moments=moments)]
    out, near, far, cot, own_rows = lax.optimization_barrier((out, near, far, cot, own_rows))
    rows_from = [own_rows]
    x = from_segment_zero(out, segment_index, sections)
    for d in range(1, sections):
        pairs = [(k, (k + d) % sections) for k in range(sections)]
        rows_from.append(lax.ppermute(own_rows, "segment", pairs))
    near_other = lax.ppermute(near, "frame", swap)
    far_other = lax.ppermute(far, "frame", swap)

    def rows_of(k):
        rows = pick(rows_from, (segment_index - k) % sections)
        bias = jnp.where(clip == 0, rows[0:1], rows[1:2])
        return bias, rows[2:3]

    cot = jnp.where(used[:, None], cot, jnp.zeros_like(cot))
    sides = halo(cot[:PLANE], cot[CELLS - PLANE :])
    small = [rows_of(k) + (places[k],) for k in range(1, sections)]
    x = jnp.pad(x, ((0, 0), (0, PITCH - WIDTH), (0, 0))).reshape(CELLS, C)
    x, on, cot, sides, small, passed = lax.optimization_barrier((x, on, cot, sides, small, passed))
    cot_before, cot_after = sides
    on_other = lax.ppermute(on, "frame", swap)
    last = lax.ppermute(passed, everyone, onward([(0, 1)], [(2, 1)]))
    fetched = (kernel, tkernel, near, near_other, far, far_other)
    sources = fetched + (on, on_other)

    skip = x
    weights = [(kernel, tkernel)]
    gains = [norm_gain]
    for k in range(1, sections):
        bias, gain, its_place = small[k - 1]
        gains.append(gain)
        if k == 1:
            hidden, low, high, stats, *taps = run(
                fetched_conv_kernel, its_place, (x, bias), CONV_OUT + TAPS, sources
            )
        else:
            joins = k == sections - 1
            args = (before, hidden, after, gathered, gains[k - 1], x, weights[k - 1][1], bias)
            args += (skip,) if joins else ()
            act, moments, x, hidden, low, high, stats, *taps = run(
                functools.partial(section_kernel, joins),
                its_place,
                args,
                (EXT, ROW8, ACT) + CONV_OUT + TAPS,
                sources,
            )
            kept[k - 1].update(act=act, moments=moments)
        weights.append(taps)
        kept.append(dict(x=x, hidden=hidden))
        if k == 2:
            low, last = lax.optimization_barrier((low, last))
        before, after = halo(low, high)
        gathered = exchange(stats)
        if k == 2:
            last_other = lax.ppermute(last, "frame", swap)
            sources = fetched + (last, last_other)

    u, u_before, u_after = cot, cot_before, cot_after
    skip_u = None
    for k in reversed(range(sections)):
        state = kept[k]
        sides = (u_before, u, u_after)
        if k == sections - 1:
            act, moments, grad, sums = run(
                functools.partial(act_grad_kernel, "last"),
                place,
                sides + (before, state["hidden"], after, gathered, gains[k], weights[k][1]),
                (EXT, ROW8, HID, STATS),
            )
            state.update(act=act, moments=moments)
        elif k == 0:
            u, grad, sums = run(
                functools.partial(act_grad_kernel, "first"),
                place,
                sides + skip_u + (state["hidden"], state["moments"], gains[k], weights[k][1]),
                (ACT, HID, STATS),
            )
        else:
            grad, sums = run(
                functools.partial(act_grad_kernel, "mid"),
                place,
                sides + (state["hidden"], state["moments"], gains[k], weights[k][1]),
                (HID, STATS),
            )
        state.update(u=u)
        sums = exchange(sums)
        args = (grad, state["hidden"], state["moments"], sums)
        if k > 0:
            hg, col, u, low, high = run(
                input_grad_kernel, place, args + (u, weights[k][0]), (ACT, ROW8, ACT, EDGE, EDGE)
            )
            u_before, u_after = halo(low, high)
            if k == sections - 1:
                skip_u = (u_before, u, u_after)
        else:
            hg, col = run(hidden_grad_kernel, place, args, (ACT, ROW8))
        state.update(hg=hg, col=col)

    partner = [(i, i ^ 1) for i in range(4)]
    keep, give = weight_grads(side_place, kept)
    got = lax.ppermute(give, "frame", swap)
    col = pick([state["col"] for state in kept], segment_index)
    other = lax.ppermute(col, "row", partner)
    chunk = ((PEERS // 2, 150, 128), BF16)
    keep, give = run(core_sum_kernel, side_place, (keep, got), (chunk, chunk))
    got = lax.ppermute(give, "row", partner)
    (summed,) = run(row_sum_kernel, side_place, (keep, got), (chunk,))
    groups = [[i for i in range(PEERS) if i % 2 == c] for c in range(2)]
    got = lax.all_to_all(summed, "frame", 0, 0, axis_index_groups=groups)
    spatial_out, temporal_out = run(
        frame_sum_kernel, side_place, (got,), (((45, C), F32), ((15, C), F32))
    )

    peers = 4 * PEERS
    gain_total = col[1] + other[1]
    totals = [jnp.where(clip == c, col[0], other[0]) for c in range(CLIPS)]
    spot = frame_index * 4 + row_index
    gain_out = lax.dynamic_slice_in_dim(gain_total, spot * (C // peers), C // peers)
    features = lax.dynamic_slice_in_dim(time_embed, spot * (TE // peers), TE // peers, axis=1)
    features = features.astype(F32)
    time_out = sum(features[c][:, None] * totals[c][None, :] for c in range(CLIPS))
    return (spatial_out[None], temporal_out[None], time_out[None], gain_out[None])


def solution(mesh):
    return jax.shard_map(
        per_device,
        mesh=mesh,
        in_specs=(
            P(None, "frame", "row", None, None),
            P(None, "frame", "row", None, None),
            P(),
            P(),
            P("segment", None, None, None),
            P("segment", None, None, None),
            P("segment", None, None),
            P("segment", None),
        ),
        out_specs=(
            P("segment", ("frame", "row"), None),
            P("segment", ("frame", "row"), None),
            P("segment", ("frame", "row"), None),
            P("segment", ("frame", "row")),
        ),
        check_vma=False,
    )
```
